32 devices in a mesh: dp: 16 (over z, y, core), seq: 2 (over x).
Axes of the slice: x: 2, y: 2, z: 4, core: 2. Of those that a mesh axis runs over, the one named last changes fastest.
Arguments:
- inputs: bfloat16 [2, 2048, 1024], P(None, ('dp', 'seq')), may hold values from -6 to 6
- cotangent: bfloat16 [2, 2048, 1024], P(None, ('dp', 'seq')), may hold values from -6 to 6
- w_qkv: bfloat16 [1024, 3072], P('dp'), may hold values from -0.1875 to 0.1875
- w_out: bfloat16 [1024, 1024], P('dp'), may hold values from -0.75 to 0.75
- w_up: bfloat16 [1024, 4096], P('dp'), may hold values from -0.1875 to 0.1875
- w_down: bfloat16 [4096, 1024], P('dp'), may hold values from -0.09375 to 0.09375
- bias_q: bfloat16 [1024], P('dp'), may hold values from -3 to 3
- bias_v: bfloat16 [1024], P('dp'), may hold values from -3 to 3
- bias_out: bfloat16 [1024], P('dp'), may hold values from -3 to 3
- gain_one: bfloat16 [1024], P('dp'), may hold values from 0.5 to 1.5
- shift_one: bfloat16 [1024], P('dp'), may hold values from -3 to 3
- bias_up: bfloat16 [4096], P('dp'), may hold values from -3 to 3
- bias_down: bfloat16 [1024], P('dp'), may hold values from -3 to 3
- gain_two: bfloat16 [1024], P('dp'), may hold values from 0.5 to 1.5
- shift_two: bfloat16 [1024], P('dp'), may hold values from -3 to 3
Outputs:
- layer_out: bfloat16 [2, 2048, 1024], P(None, ('dp', 'seq'))
- input_grad: float32 [2, 2048, 1024], P(None, ('dp', 'seq'))
- grad_qkv: float32 [1024, 3072], P('dp')
- grad_out: float32 [1024, 1024], P('dp')
- grad_up: float32 [1024, 4096], P('dp')
- grad_down: float32 [4096, 1024], P('dp')
- grad_bias_q: float32 [1024], P('dp')
- grad_bias_v: float32 [1024], P('dp')
- grad_bias_out: float32 [1024], P('dp')
- grad_gain_one: float32 [1024], P('dp')
- grad_shift_one: float32 [1024], P('dp')
- grad_bias_up: float32 [4096], P('dp')
- grad_bias_down: float32 [1024], P('dp')
- grad_gain_two: float32 [1024], P('dp')
- grad_shift_two: float32 [1024], P('dp')
The draws below stay inside these ranges and needn't reach their ends.
All inputs are finite; a program needn't handle non-finite values.
Results may differ from the reference program's by a relative error of at most 0.015.
Values may be sent and summed in bfloat16 or wider, within the bound.
No kernel may reach another device: no remote copies, remote signals or barrier semaphores. Data moves between devices by JAX's collectives and lax.ppermute only.
A program may use at most 192 MiB of HBM per device.

```python
import math
import jax
import jax.numpy as jnp
from jax import lax

D = 1024
HEADS = 16
HEAD = 64
FF = 4096
MICRO = 2
SEQS = 16
LEN = 128
MB_TOKENS = 2048


def block_levels(key, extent, split, least, high):
    def one(position, blocks):
        draws = jax.random.uniform(jax.random.fold_in(jax.random.fold_in(key, 6), position), (blocks,), jnp.float32, least / len(split), high / len(split))
        return jnp.repeat(jnp.exp(draws), extent[position] // blocks).reshape((-1,) + (1,) * (len(extent) - position - 1))

    level = one(*split[0])
    for cut in split[1:]:
        level = level * one(*cut)
    return level


def scatter_about(rng, shape, scale, most, split=(), dtype=jnp.bfloat16):
    drawn = scale * jax.random.normal(rng, shape, jnp.float32)
    if split:
        drawn = drawn * block_levels(rng, shape, split, -0.22, 0.18)
    return jnp.clip(drawn, -most, most).astype(dtype)


def setup_inputs(seed: int = 0) -> dict:
    seeds = jax.random.split(jax.random.key(seed), 16)
    inputs = scatter_about(seeds[0], (MICRO, MB_TOKENS, D), 1.0, 6.0, ((1, 32),))
    cotangent = scatter_about(seeds[1], (MICRO, MB_TOKENS, D), 1.0, 6.0, ((1, 32),))
    w_qkv = scatter_about(seeds[2], (D, 3 * D), D ** -0.5, 0.1875, ((0, 16),))
    w_out = scatter_about(seeds[3], (D, D), (D // 16) ** -0.5, 0.75, ((0, 16),))
    w_up = scatter_about(seeds[4], (D, FF), D ** -0.5, 0.1875, ((0, 16),))
    w_down = scatter_about(seeds[5], (FF, D), FF ** -0.5, 0.09375, ((0, 16),))
    bias_q = scatter_about(seeds[6], (D,), 0.5, 3.0, ((0, 16),))
    bias_v = scatter_about(seeds[7], (D,), 0.5, 3.0, ((0, 16),))
    bias_out = scatter_about(seeds[8], (D,), 0.5, 3.0, ((0, 16),))
    gain_one = jnp.clip(1.0 + 0.1 * jax.random.normal(seeds[9], (D,), jnp.float32), 0.5, 1.5).astype(jnp.bfloat16)
    shift_one = scatter_about(seeds[10], (D,), 0.5, 3.0, ((0, 16),))
    bias_up = scatter_about(seeds[11], (FF,), 0.5, 3.0, ((0, 16),))
    bias_down = scatter_about(seeds[12], (D,), 0.5, 3.0, ((0, 16),))
    gain_two = jnp.clip(1.0 + 0.1 * jax.random.normal(seeds[13], (D,), jnp.float32), 0.5, 1.5).astype(jnp.bfloat16)
    shift_two = scatter_about(seeds[14], (D,), 0.5, 3.0, ((0, 16),))
    return {"inputs": inputs, "cotangent": cotangent, "w_qkv": w_qkv, "w_out": w_out, "w_up": w_up, "w_down": w_down, "bias_q": bias_q, "bias_v": bias_v, "bias_out": bias_out, "gain_one": gain_one, "shift_one": shift_one, "bias_up": bias_up, "bias_down": bias_down, "gain_two": gain_two, "shift_two": shift_two}


@jax.custom_vjp
def low(v):
    return lax.optimization_barrier(v.astype(jnp.bfloat16)).astype(jnp.float32)

@jax.custom_vjp
def low_back(v):
    return v

def low_keep(v):
    return (low(v), None)

def low_pass(kept, grad):
    return (grad,)

def back_keep(v):
    return (v, None)

def back_low(kept, grad):
    return (low(grad),)
low.defvjp(low_keep, low_pass)
low_back.defvjp(back_keep, back_low)

def normalize(features, gain, shift):
    centre = lax.optimization_barrier(jnp.mean(features, axis=-1, keepdims=True))
    centred = features - centre
    spread = lax.optimization_barrier(jnp.mean(centred * centred, axis=-1, keepdims=True))
    return centred * lax.rsqrt(spread + 1e-12) * gain + shift

def gelu_exact(values):
    return 0.5 * values * (1.0 + jax.scipy.special.erf(values * (1.0 / math.sqrt(2.0))))

def layer(params, blocks):
    w_qkv, w_out, w_up, w_down, bias_q, bias_v, bias_out, gain_one, shift_one, bias_up, bias_down, gain_two, shift_two = params
    high = lax.Precision.HIGHEST
    group, length, width = blocks.shape
    rows = blocks.reshape(-1, width)
    qkv = jnp.dot(rows, w_qkv, precision=high)
    queries = low_back(low(qkv[:, :width] + bias_q))
    keys = low_back(low(qkv[:, width:2 * width]))
    values = low_back(low(qkv[:, 2 * width:] + bias_v))
    shaped = (group, length, HEADS, HEAD)
    scores = jnp.einsum('gqhd,gkhd->ghqk', queries.reshape(shaped), keys.reshape(shaped), precision=high) * (1.0 / math.sqrt(HEAD))
    scores = low_back(scores)
    shifted = scores - lax.optimization_barrier(jnp.max(scores, axis=-1, keepdims=True))
    expo = jnp.exp(shifted)
    probs = expo / lax.optimization_barrier(jnp.sum(expo, axis=-1, keepdims=True))
    context = jnp.einsum('ghqk,gkhd->gqhd', low(probs), values.reshape(shaped), precision=high).reshape(-1, width)
    context = low_back(low(context))
    attended = low_back(jnp.dot(context, w_out, precision=high) + bias_out)
    first = normalize(rows + attended, gain_one, shift_one)
    pre_act = low_back(jnp.dot(low(first), w_up, precision=high) + bias_up)
    act = low(gelu_exact(pre_act))
    mlp = low_back(jnp.dot(act, w_down, precision=high) + bias_down)
    second = normalize(first + mlp, gain_two, shift_two)
    return second.reshape(group, length, width)

def add_up(first_term, second_term):
    return first_term + second_term

def reference(inputs, cotangent, w_qkv, w_out, w_up, w_down, bias_q, bias_v, bias_out, gain_one, shift_one, bias_up, bias_down, gain_two, shift_two):
    params = tuple((weight.astype(jnp.float32) for weight in (w_qkv, w_out, w_up, w_down, bias_q, bias_v, bias_out, gain_one, shift_one, bias_up, bias_down, gain_two, shift_two)))
    count = MICRO * SEQS
    group = math.gcd(count, 16)
    blocks = inputs.astype(jnp.float32).reshape(count // group, group, LEN, D)
    upstream = cotangent.astype(jnp.float32).reshape(count // group, group, LEN, D)

    def step(total, item):
        block, upward = item
        result, pull = jax.vjp(layer, params, block)
        grad_params, grad_block = pull(upward)
        return (jax.tree.map(add_up, total, grad_params), (result, grad_block))
    zeros = tuple((jnp.zeros_like(weight) for weight in params))
    totals, (results, grad_blocks) = lax.scan(step, zeros, (blocks, upstream))
    layer_out = results.reshape(MICRO, MB_TOKENS, D).astype(jnp.bfloat16)
    input_grad = grad_blocks.reshape(MICRO, MB_TOKENS, D).astype(jnp.float32)
    return (layer_out, input_grad, totals[0], totals[1], totals[2], totals[3], totals[4], totals[5], totals[6], totals[7], totals[8], totals[9], totals[10], totals[11], totals[12])
```

```python
import math

import jax
import jax.numpy as jnp
from jax import lax
from jax.sharding import PartitionSpec as P

HEAD = 64
CORES = 2
LONGEST = 16
SHORT = jnp.bfloat16
WIDE = jnp.float32


def normalize(features, gain, shift):
    centre = jnp.mean(features, axis=-1, keepdims=True)
    centred = features - centre
    spread = jnp.mean(centred * centred, axis=-1, keepdims=True)
    return centred * lax.rsqrt(spread + 1e-12) * gain + shift


def gelu_exact(values):
    return 0.5 * values * (1.0 + lax.erf(values * (1.0 / math.sqrt(2.0))))


def gelu_slope(values):
    bell = jnp.exp(values * values * -0.5) * (1.0 / math.sqrt(2.0 * math.pi))
    return 0.5 * (1.0 + lax.erf(values * (1.0 / math.sqrt(2.0)))) + values * bell


def times(left, right):
    return jnp.dot(left, right, preferred_element_type=WIDE)


def times_back(left, right):
    return lax.dot_general(left, right, (((1,), (1,)), ((), ())), preferred_element_type=WIDE)


def inner_rows(left, right):
    return lax.dot_general(left, right, (((0,), (0,)), ((), ())), preferred_element_type=WIDE)


def pick(array, index, axis):
    return lax.dynamic_index_in_dim(array, index, axis, keepdims=False)


def in_order(place, own, other, axis):
    first = place == 0
    return jnp.stack([jnp.where(first, own, other), jnp.where(first, other, own)], axis=axis)


def ring_order(chips):
    half = chips // 2
    return [2 * i for i in range(half)] + [2 * i + 1 for i in reversed(range(half))]


def build(mesh):
    devices = mesh.shape["dp"]
    chips = devices // CORES
    ring = ring_order(chips)
    place_of = [ring.index(chip) for chip in range(chips)]

    def hop(step):
        return [
            (ring[i] * CORES + core, ring[(i + step) % chips] * CORES + core)
            for i in range(chips)
            for core in range(CORES)
        ]

    onward, backward = hop(1), hop(-1)
    same_core = [list(range(core, devices, CORES)) for core in range(CORES)]
    core_pairs = [(i, i ^ 1) for i in range(devices)]

    def swap_core(array):
        return lax.ppermute(array, "dp", core_pairs)

    def swap_seq(array):
        return lax.ppermute(array, "seq", [(0, 1), (1, 0)])

    def per_device(
        inputs,
        cotangent,
        w_qkv,
        w_out,
        w_up,
        w_down,
        bias_q,
        bias_v,
        bias_out,
        gain_one,
        shift_one,
        bias_up,
        bias_down,
        gain_two,
        shift_two,
    ):
        index = lax.axis_index("dp")
        core = index % CORES
        chip = index // CORES
        half = lax.axis_index("seq")
        spot = jnp.asarray(place_of)[chip]
        ring_table = jnp.asarray(ring)

        def at(offset):
            return ring_table[(spot + offset + chips) % chips]

        def gather_ring(chunk, flip):
            if chips > LONGEST:
                whole = lax.all_gather(chunk, "dp", axis_index_groups=same_core)
                return whole
            far, near = (backward, onward) if flip else (onward, backward)
            sign = -1 if flip else 1
            whole = jnp.zeros((chips,) + chunk.shape, chunk.dtype)
            whole = lax.dynamic_update_index_in_dim(whole, chunk, chip, 0)
            one = two = chunk
            for step in range(1, chips // 2 + 1):
                one = lax.ppermute(one, "dp", far)
                whole = lax.dynamic_update_index_in_dim(whole, one, at(-sign * step), 0)
                if step < chips // 2:
                    two = lax.ppermute(two, "dp", near)
                    whole = lax.dynamic_update_index_in_dim(whole, two, at(sign * step), 0)
            return whole

        def sum_ring(parts, flip):
            if chips > LONGEST:
                parts = parts.astype(SHORT)
                return lax.psum_scatter(parts, "dp", axis_index_groups=same_core).astype(WIDE)
            far, near = (backward, onward) if flip else (onward, backward)
            sign = -1 if flip else 1

            def part(offset):
                return pick(parts, at(offset), 0).astype(WIDE)

            def run(perm, direction, distance):
                moving = part(direction * distance).astype(SHORT)
                for step in range(distance - 1, -1, -1):
                    moving = lax.ppermute(moving, "dp", perm)
                    if step:
                        moving = (moving.astype(WIDE) + part(direction * step)).astype(SHORT)
                return moving.astype(WIDE)

            return run(far, sign, chips // 2) + run(near, -sign, chips // 2 - 1) + part(0)

        micro, rows, width = inputs.shape
        depth = w_qkv.shape[0]
        units = w_down.shape[0]
        tall = w_up.shape[1]
        quarter = width // 4
        heads = quarter // HEAD
        group = 4 * micro * rows
        scale = 1.0 / math.sqrt(HEAD)
        my_quarter = 2 * half + core

        def share_tokens(own):
            pair = jnp.concatenate([own, swap_seq(own)], axis=1)
            return jnp.concatenate([pair, swap_core(pair)], axis=0).reshape(group, -1)

        def sum_tokens(partial):
            parts = partial.reshape(2, micro, 2, rows, -1)
            mine = parts[0] + swap_core(parts[1].astype(SHORT)).astype(WIDE)
            return mine[:, 0] + swap_seq(mine[:, 1].astype(SHORT)).astype(WIDE)

        vectors = (
            bias_q,
            bias_v,
            bias_out,
            gain_one,
            shift_one,
            bias_down,
            gain_two,
            shift_two,
            bias_up,
        )
        packed = jnp.concatenate(vectors)
        slim = packed.shape[0]
        row = jnp.pad(packed, (0, 3 * quarter - slim)).reshape(1, -1)

        by_quarter = w_qkv.reshape(depth, 3, 2, 2, quarter)
        by_quarter = pick(by_quarter, half, 2)
        mine = pick(by_quarter, core, 2).reshape(depth, 3 * quarter)
        theirs = pick(by_quarter, 1 - core, 2).reshape(depth, 3 * quarter)
        mine = jnp.concatenate([mine, row], axis=0)
        theirs = jnp.concatenate([theirs, row], axis=0)
        both = in_order(core, mine, swap_core(theirs), 0)
        flat = jnp.concatenate([both[:, :depth].reshape(2 * depth, -1), both[:, depth]], axis=0)
        flat = jnp.pad(flat, ((0, 14), (0, 0)))
        qkv_all = gather_ring(flat, False)
        full_qkv = qkv_all[:, : 2 * depth].reshape(width, 3 * quarter)
        vector_all = qkv_all[:, 2 * depth : 2 * depth + 2, :slim].reshape(devices, slim).astype(WIDE)

        out_all = gather_ring(w_out, True)
        full_out = in_order(core, out_all, swap_core(out_all), 1).reshape(width, width)

        by_unit = w_up.reshape(depth, chips, 2, 2, units // 2)
        by_unit = pick(by_unit, half, 3)
        mine = pick(by_unit, core, 2).reshape(depth, tall // 4)
        theirs = pick(by_unit, 1 - core, 2).reshape(depth, tall // 4)
        both = in_order(core, mine, swap_core(theirs), 0).reshape(2 * depth, tall // 4)
        full_up = gather_ring(both, False).reshape(width, tall // 4)

        own_down = pick(w_down.reshape(2, units // 2, width), half, 0)
        full_down = gather_ring(own_down, True).reshape(tall // 4, width)

        tokens = share_tokens(inputs)

        (
            query_bias,
            value_bias,
            out_bias,
            first_gain,
            first_shift,
            down_bias,
            second_gain,
            second_shift,
        ) = [vector_all[:, i * depth : (i + 1) * depth].reshape(-1) for i in range(8)]
        up_bias = vector_all[:, 8 * depth :].reshape(chips, 2, 2, units // 2)
        up_bias = pick(pick(up_bias, core, 1), half, 1).reshape(-1)
        query_bias = pick(query_bias.reshape(4, quarter), my_quarter, 0)
        value_bias = pick(value_bias.reshape(4, quarter), my_quarter, 0)

        qkv = times(tokens, full_qkv)
        shaped = (2 * micro, 2 * rows, heads, HEAD)
        queries = (qkv[:, :quarter] + query_bias).astype(SHORT).reshape(shaped)
        keys = qkv[:, quarter : 2 * quarter].astype(SHORT).reshape(shaped)
        values = (qkv[:, 2 * quarter :] + value_bias).astype(SHORT).reshape(shaped)
        scores = jnp.einsum("sqhd,skhd->shqk", queries, keys, preferred_element_type=WIDE) * scale
        top = jnp.max(scores, axis=-1, keepdims=True)
        expo = jnp.exp(scores - top)
        probs = expo / jnp.sum(expo, axis=-1, keepdims=True)
        probs_low = probs.astype(SHORT)
        context = jnp.einsum("shqk,skhd->sqhd", probs_low, values, preferred_element_type=WIDE)
        context = context.astype(SHORT).reshape(2, micro, 2, rows, quarter)

        from_seq = swap_seq(context[:, :, 1])
        context = in_order(half, context[:, :, 0], from_seq, 3)
        from_core = swap_core(context[1])
        context = in_order(core, context[0], from_core, 3).reshape(micro * rows, width)

        attended = times(context, full_out) + out_bias
        resid_one = inputs.reshape(micro * rows, width).astype(WIDE) + attended
        first, pull_one = jax.vjp(normalize, resid_one, first_gain, first_shift)
        first_low = share_tokens(first.astype(SHORT).reshape(micro, rows, width))
        pre_act = times(first_low, full_up) + up_bias
        act = gelu_exact(pre_act).astype(SHORT)
        mlp = sum_tokens(times(act, full_down)).reshape(micro * rows, width) + down_bias
        second, pull_two = jax.vjp(normalize, first + mlp, second_gain, second_shift)
        layer_out = second.astype(SHORT).reshape(inputs.shape)

        incoming = cotangent.reshape(micro * rows, width).astype(WIDE)
        grad_resid_two, grad_gain_b, grad_shift_b = pull_two(incoming)
        own_mlp = grad_resid_two.astype(SHORT)
        grad_mlp = share_tokens(own_mlp.reshape(micro, rows, width))
        grad_down = inner_rows(act, grad_mlp)
        down_share = sum_ring(grad_down.reshape(chips, units // 2, width), True)
        grad_pre = (times_back(grad_mlp, full_down) * gelu_slope(pre_act)).astype(SHORT)
        grad_up = inner_rows(first_low, grad_pre)
        up_share = sum_ring(grad_up.reshape(chips, 2 * depth, tall // 4), False)
        back = sum_tokens(times_back(grad_pre, full_up)).reshape(micro * rows, width)
        grad_resid_one, grad_gain_a, grad_shift_a = pull_one(grad_resid_two + back)
        grad_attended = grad_resid_one.astype(SHORT)
        grad_out = inner_rows(context, grad_attended).reshape(chips, 2, depth, width)
        grad_out = pick(grad_out, core, 1) + swap_core(
            pick(grad_out, 1 - core, 1).astype(SHORT)
        ).astype(WIDE)
        out_share = sum_ring(grad_out, True)

        grad_context = times_back(grad_attended, full_out).astype(SHORT)
        grad_context = grad_context.reshape(micro, rows, 2, 2, quarter)
        from_core = swap_core(pick(grad_context, 1 - core, 3))
        grad_context = jnp.stack([pick(grad_context, core, 3), from_core], axis=0)
        from_seq = swap_seq(pick(grad_context, 1 - half, 3))
        grad_context = jnp.stack([pick(grad_context, half, 3), from_seq], axis=2).reshape(shaped)

        grad_probs = jnp.einsum("sqhd,skhd->shqk", grad_context, values, preferred_element_type=WIDE)
        grad_scores = (
            probs * (grad_probs - jnp.sum(probs * grad_probs, axis=-1, keepdims=True))
        ).astype(SHORT)
        grad_queries = (
            jnp.einsum("shqk,skhd->sqhd", grad_scores, keys, preferred_element_type=WIDE) * scale
        ).astype(SHORT)
        grad_keys = (
            jnp.einsum("shqk,sqhd->skhd", grad_scores, queries, preferred_element_type=WIDE) * scale
        ).astype(SHORT)
        grad_values = jnp.einsum(
            "shqk,sqhd->skhd", probs_low, grad_context, preferred_element_type=WIDE
        ).astype(SHORT)
        grad_tokens = jnp.concatenate(
            [part.reshape(group, quarter) for part in (grad_queries, grad_keys, grad_values)], axis=1
        )
        input_grad = sum_tokens(times_back(grad_tokens, full_qkv)).reshape(micro * rows, width)
        input_grad = (grad_resid_one + input_grad).reshape(inputs.shape)

        def column_sum(part):
            return jnp.sum(part.astype(WIDE), axis=0)

        token_sums = column_sum(grad_tokens).reshape(3, quarter)
        spread_q = lax.dynamic_update_index_in_dim(
            jnp.zeros((4, quarter), WIDE), token_sums[0], my_quarter, 0
        )
        spread_v = lax.dynamic_update_index_in_dim(
            jnp.zeros((4, quarter), WIDE), token_sums[2], my_quarter, 0
        )
        spread_up = lax.dynamic_update_slice(
            jnp.zeros((chips, 2, 2, units // 2), WIDE),
            column_sum(grad_pre).reshape(chips, 1, 1, units // 2),
            (0, core, half, 0),
        )
        sums = (
            spread_q,
            spread_v,
            column_sum(grad_attended),
            grad_gain_a,
            grad_shift_a,
            column_sum(own_mlp),
            grad_gain_b,
            grad_shift_b,
        )
        lines = jnp.concatenate(
            [part.reshape(devices, depth) for part in sums] + [spread_up.reshape(devices, units)],
            axis=1,
        )
        lines = jnp.pad(lines, ((0, 0), (0, 3 * quarter - slim))).reshape(chips, 2, 3 * quarter)
        lines = jnp.pad(lines, ((0, 0), (0, 14), (0, 0)))
        grad_qkv = inner_rows(tokens, grad_tokens).reshape(chips, 2 * depth, 3 * quarter)
        qkv_share = sum_ring(jnp.concatenate([grad_qkv, lines], axis=1), False)

        def to_owner(share, kept_rows):
            split = share.reshape(2, kept_rows, -1).astype(SHORT)
            own, other = pick(split, core, 0), swap_core(pick(split, 1 - core, 0))
            return own, other

        own, other = to_owner(up_share, depth)
        up_pair = in_order(core, own.reshape(depth, chips, -1), other.reshape(depth, chips, -1), 2)
        up_pair = in_order(half, up_pair, swap_seq(up_pair), 3)
        final_up = up_pair.reshape(depth, tall).astype(WIDE)

        down_short = down_share.astype(SHORT)
        final_down = in_order(half, down_short, swap_seq(down_short), 0)
        final_down = final_down.reshape(units, width).astype(WIDE)

        final_out = out_share + swap_seq(out_share.astype(SHORT)).astype(WIDE)

        split = qkv_share[: 2 * depth].reshape(2, depth, -1)
        line = qkv_share[2 * depth : 2 * depth + 2].reshape(2, 1, -1)
        split = jnp.concatenate([split, line], axis=1).astype(SHORT)
        own, other = pick(split, core, 0), swap_core(pick(split, 1 - core, 0))
        pair = in_order(
            core, own[:depth].reshape(depth, 3, quarter), other[:depth].reshape(depth, 3, quarter), 2
        )
        line = own[depth:].astype(WIDE) + other[depth:].astype(WIDE)
        pair_flat = pair.reshape(depth, 6 * quarter)
        line_flat = jnp.pad(line.astype(SHORT), ((0, 0), (0, 3 * quarter)))
        sent = swap_seq(jnp.concatenate([pair_flat, line_flat], axis=0))
        pair = in_order(half, pair, sent[:depth].reshape(depth, 3, 2, quarter), 2)
        final_qkv = pair.reshape(depth, 3 * width).astype(WIDE)
        line = (line + sent[depth:, : 3 * quarter].astype(WIDE)).reshape(-1)[:slim]
        finals = [line[i * depth : (i + 1) * depth] for i in range(8)] + [line[8 * depth :]]

        return (
            layer_out,
            input_grad,
            final_qkv,
            final_out,
            final_up,
            final_down,
            finals[0],
            finals[1],
            finals[2],
            finals[3],
            finals[4],
            finals[8],
            finals[5],
            finals[6],
            finals[7],
        )

    return per_device


def solution(mesh):
    token = P(None, ("dp", "seq"), None)
    matrix = P("dp", None)
    vector = P("dp")
    placed = (token, token) + (matrix,) * 4 + (vector,) * 9
    return jax.shard_map(
        build(mesh), mesh=mesh, in_specs=placed, out_specs=placed, check_vma=False
    )
```

```python
import functools
import math

import jax
import jax.numpy as jnp
from jax import lax
from jax.experimental import pallas as pl
from jax.experimental.pallas import tpu as pltpu
from jax.sharding import PartitionSpec as P

HEAD = 64
CORES = 2
PARTS = 8
SHORT = jnp.bfloat16
WIDE = jnp.float32
LIMIT = 56 * 1024 * 1024
LINES = 16
LANES = 256


def gelu_exact(values):
    return 0.5 * values * (1.0 + lax.erf(values * (1.0 / math.sqrt(2.0))))


def gelu_slope(values):
    bell = jnp.exp(values * values * -0.5) * (1.0 / math.sqrt(2.0 * math.pi))
    return 0.5 * (1.0 + lax.erf(values * (1.0 / math.sqrt(2.0)))) + values * bell


def times(left, right):
    return jnp.dot(left, right, preferred_element_type=WIDE)


def times_back(left, right):
    return lax.dot_general(left, right, (((1,), (1,)), ((), ())), preferred_element_type=WIDE)


def inner_rows(left, right):
    return lax.dot_general(left, right, (((0,), (0,)), ((), ())), preferred_element_type=WIDE)


def column_sum(part):
    return jnp.sum(part, axis=0, keepdims=True)


def standard(features):
    centre = jnp.mean(features, axis=-1, keepdims=True)
    centred = features - centre
    spread = jnp.mean(centred * centred, axis=-1, keepdims=True)
    slope = lax.rsqrt(spread + 1e-12)
    return centred * slope, slope


def standard_back(normal, slope, grad):
    even = jnp.mean(grad, axis=-1, keepdims=True)
    along = jnp.mean(normal * grad, axis=-1, keepdims=True)
    return slope * (grad - even - normal * along)


def pick(array, index, axis):
    return lax.dynamic_index_in_dim(array, index, axis, keepdims=False)


def in_order(place, own, other, axis):
    first = place == 0
    return jnp.stack([jnp.where(first, own, other), jnp.where(first, other, own)], axis=axis)


def block(index, size):
    return pl.ds(pl.multiple_of(index * size, size), size)


def here():
    index = lax.axis_index("dp")
    return lax.div(index, CORES), lax.rem(index, CORES), lax.axis_index("seq")


def part_index(step, flip, ringed, chip, chips):
    if not ringed:
        return step
    half = chips // 2
    upper = lax.rem(chip, 2)
    level = lax.div(chip, 2)
    spot = jnp.where(upper == 0, level, chips - 1 - level)
    away = (step + 1) // 2
    sign = -1 if (step % 2 == 1) != flip else 1
    spot = lax.rem(spot + sign * away + chips, chips)
    return jnp.where(spot < half, 2 * spot, 2 * (chips - 1 - spot) + 1)


def call(body, outs, scratch=(), flops=0, moved=0):
    return pl.pallas_call(
        body,
        out_shape=[jax.ShapeDtypeStruct(shape, kind) for shape, kind in outs],
        scratch_shapes=[pltpu.VMEM(shape, kind) for shape, kind in scratch],
        compiler_params=pltpu.CompilerParams(vmem_limit_bytes=LIMIT),
        cost_estimate=pl.CostEstimate(flops=flops, bytes_accessed=moved, transcendentals=0),
    )


def pack_kernel(*refs):
    vectors, up_bias, w_qkv, w_out, mine, theirs = refs[:8], *refs[8:]
    _, core, half = here()
    depth = w_qkv.shape[0]
    width = w_out.shape[1]
    quarter = width // 4
    for out, which in ((mine, core), (theirs, 1 - core)):
        for third in range(3):
            start = third * width + (2 * half + which) * quarter
            out[:depth, third * quarter : (third + 1) * quarter] = w_qkv[
                :, pl.ds(pl.multiple_of(start, quarter), quarter)
            ]
        out[:depth, 3 * quarter :] = w_out[:, block(which, width // 2)]
        lines = [
            jnp.pad(vector[...], ((0, 0), (0, LANES - depth))).astype(WIDE) for vector in vectors
        ]
        lines.append(jnp.pad(up_bias[...].astype(WIDE), ((0, 0), (0, LANES - up_bias.shape[1]))))
        lines.append(jnp.zeros((LINES - 9, LANES), WIDE))
        out[depth:, :LANES] = jnp.concatenate(lines, axis=0).astype(SHORT)
        out[depth:, LANES:] = jnp.zeros((LINES, out.shape[1] - LANES), SHORT)


def heads_of(qkv, rows, head, quarter):
    return [
        qkv[rows, third * quarter + head * HEAD : third * quarter + (head + 1) * HEAD]
        for third in range(3)
    ]


def softmax(queries, keys, scale):
    scores = times_back(queries, keys) * scale
    expo = jnp.exp(scores - jnp.max(scores, axis=-1, keepdims=True))
    return expo / jnp.sum(expo, axis=-1, keepdims=True)


def fill_group(group, pieces, micro):
    rows = pieces[0].shape[0] // micro
    for place in range(4 * micro):
        far, item, side = place // (2 * micro), place // 2 % micro, place % 2
        group[place * rows : (place + 1) * rows, :] = pieces[2 * far + side][
            item * rows : (item + 1) * rows, :
        ]


def attention_kernel(micro, where, *refs):
    pieces, chunks, rest = refs[:4], refs[4:12], refs[12:]
    tokens, full, qkv, keep, send, vectors, up_bias, out_half, wide = rest
    chip, core, half = here()
    quarter = keep.shape[1]
    scale = 1.0 / math.sqrt(HEAD)
    fill_group(tokens, pieces, micro)
    for step in range(PARTS):
        spot = block(where(step, chip), 128)
        chunk = chunks[step]
        full[spot, :] = chunk[:128, : 3 * quarter]
        out_half[spot, :] = chunk[:128, 3 * quarter :]
        lines = jnp.concatenate([chunk[128:, :64], chunk[128:, LANES : LANES + 64]], axis=1)
        vectors[:, spot] = lines.astype(WIDE)
        lines = chunk[128:, block(core * (LANES // 128) + half, 128)]
        up_bias[:, spot] = lines.astype(WIDE)[8:9, :]
    wide[...] = times(tokens[...], full[...])
    spot = block(2 * half + core, quarter)
    qkv[:, :quarter] = (wide[:, :quarter] + vectors[0:1, spot]).astype(SHORT)
    qkv[:, quarter : 2 * quarter] = wide[:, quarter : 2 * quarter].astype(SHORT)
    qkv[:, 2 * quarter :] = (wide[:, 2 * quarter :] + vectors[1:2, spot]).astype(SHORT)
    length = tokens.shape[0] // (2 * micro)
    rows = length // 2
    for item in range(2 * micro):
        for pair in range(quarter // 128):
            both = []
            for head in (2 * pair, 2 * pair + 1):
                queries, keys, values = heads_of(
                    qkv, slice(item * length, (item + 1) * length), head, quarter
                )
                probs = softmax(queries, keys, scale).astype(SHORT)
                both.append(times(probs, values))
            both = jnp.concatenate(both, axis=1).astype(SHORT)
            spot = slice(pair * 128, (pair + 1) * 128)
            keep[item * rows : (item + 1) * rows, spot] = both[:rows]
            send[item * rows : (item + 1) * rows, spot] = both[rows:]


def first_kernel(
    inputs, keep, from_seq, from_core, mine, other, vectors, resid, first, low, context
):
    _, core, half = here()
    rows, width = inputs.shape
    quarter = width // 4
    flip_core, flip_half = 1 - core, 1 - half
    context[:, block(2 * half + core, quarter)] = keep[:rows, :]
    context[:, block(2 * flip_half + core, quarter)] = from_seq[:rows, :]
    context[:, block(2 * half + flip_core, quarter)] = from_core[:, :quarter]
    context[:, block(2 * flip_half + flip_core, quarter)] = from_core[:, quarter:]
    whole = context[...]
    resid[:, block(core, width // 2)] = times(whole, mine[...])
    resid[:, block(flip_core, width // 2)] = times(whole, other[...])
    features = inputs[...].astype(WIDE) + (resid[...] + vectors[2:3, :])
    resid[...] = features
    normal, _ = standard(features)
    features = normal * vectors[3:4, :] + vectors[4:5, :]
    first[...] = features
    low[...] = features.astype(SHORT)


def split_rows(value, start, micro, rows, keep, send):
    for place in range(value.shape[0] // rows):
        far, item, side = (
            (start + place * rows) // rows // (2 * micro),
            (start + place * rows) // rows // 2 % micro,
            (start + place * rows) // rows % 2,
        )
        part = value[place * rows : (place + 1) * rows, :]
        if far:
            send[side, item * rows : (item + 1) * rows, :] = part.astype(SHORT)
        else:
            keep[side, item * rows : (item + 1) * rows, :] = part


def forward_kernel(micro, where, *refs):
    pieces, chunks, up_bias, rest = refs[:4], refs[4:12], refs[12], refs[13:]
    group, full_up, full_down, pre_act, act, keep, send = rest
    chip, _, _ = here()
    fill_group(group, pieces, micro)
    for step in range(PARTS):
        spot = block(where(step, chip), 128)
        full_up[spot, :] = chunks[step][:128, :]
        full_down[spot, :] = chunks[step][128:, :]
    rows = pieces[0].shape[0] // micro
    tall = group.shape[0] // 2
    for side in range(2):
        spot = slice(side * tall, (side + 1) * tall)
        pre = times(group[spot, :], full_up[...]) + up_bias[...]
        pre_act[spot, :] = pre
        act[spot, :] = gelu_exact(pre).astype(SHORT)
        out = times(act[spot, :], full_down[...])
        split_rows(out, side * tall, micro, rows, keep, send)


def second_kernel(
    first, keep, from_core, from_seq, vectors, cotangent, out, grad, low, sums
):
    mlp = keep[0] + from_core[0].astype(WIDE) + from_seq[...].astype(WIDE)
    normal, slope = standard(first[...] + (mlp + vectors[5:6, :]))
    out[...] = (normal * vectors[6:7, :] + vectors[7:8, :]).astype(SHORT)
    incoming = cotangent[...].astype(WIDE)
    resid = standard_back(normal, slope, incoming * vectors[6:7, :])
    grad[...] = resid
    short = resid.astype(SHORT)
    low[...] = short
    sums[...] = jnp.zeros_like(sums)
    sums[0:1, :] = column_sum(short.astype(WIDE))
    sums[1:2, :] = column_sum(incoming * normal)
    sums[2:3, :] = column_sum(incoming)


def backward_kernel(micro, where, *refs):
    pieces, rest = refs[:4], refs[4:]
    group, full_up, full_down, pre_act, act, chunks, keep, send, sums, grad, pre = rest
    chip, _, _ = here()
    fill_group(grad, pieces, micro)
    rows = pieces[0].shape[0] // micro
    tall = grad.shape[0] // 2
    total = None
    for side in range(2):
        spot = slice(side * tall, (side + 1) * tall)
        slope = gelu_slope(pre_act[spot, :])
        part = (times_back(grad[spot, :], full_down[...]) * slope).astype(SHORT)
        pre[spot, :] = part
        part = column_sum(part.astype(WIDE))
        total = part if total is None else total + part
    sums[...] = total
    for step in range(PARTS):
        spot = block(where(step, chip), 128)
        chunks[step, 128:, :] = inner_rows(act[:, spot], grad[...]).astype(SHORT)
        chunks[step, :128, :] = inner_rows(group[:, spot], pre[...]).astype(SHORT)
    for side in range(2):
        spot = slice(side * tall, (side + 1) * tall)
        out = times_back(pre[spot, :], full_up[...])
        split_rows(out, side * tall, micro, rows, keep, send)


def first_back_kernel(
    resid,
    grad_two,
    keep,
    from_core,
    from_seq,
    vectors,
    context,
    mine,
    other,
    grad,
    out_keep,
    out_send,
    ctx_keep,
    ctx_send,
    sums,
):
    _, core, half = here()
    width = resid.shape[1]
    quarter = width // 4
    incoming = grad_two[...] + (keep[0] + from_core[0].astype(WIDE) + from_seq[...].astype(WIDE))
    normal, slope = standard(resid[...])
    value = standard_back(normal, slope, incoming * vectors[3:4, :])
    grad[...] = value
    short = value.astype(SHORT)
    sums[...] = jnp.zeros_like(sums)
    sums[0:1, :] = column_sum(short.astype(WIDE))
    sums[1:2, :] = column_sum(incoming * normal)
    sums[2:3, :] = column_sum(incoming)
    left, right = short[:, : width // 2], short[:, width // 2 :]
    own = jnp.where(core == 0, left, right)
    away = jnp.where(core == 0, right, left)
    out_keep[...] = inner_rows(context[...], own)
    out_send[...] = inner_rows(context[...], away).astype(SHORT)
    for target, which in ((ctx_keep, core), (ctx_send, 1 - core)):
        for side, which_half in enumerate((half, 1 - half)):
            spot = block(2 * which_half + which, quarter)
            value = times_back(own, mine[spot, :]) + times_back(away, other[spot, :])
            target[:, side * quarter : (side + 1) * quarter] = value.astype(SHORT)


def attention_back_kernel(micro, where, *refs):
    qkv, ctx_keep, ctx_core, ctx_seq, tokens, full, out_keep, out_core = refs[:8]
    sums_two, sums_one, up_sums, chunks, keep, send, grad, vectors = refs[8:]
    chip, core, half = here()
    quarter = qkv.shape[1] // 3
    length = qkv.shape[0] // (2 * micro)
    rows = length // 2
    scale = 1.0 / math.sqrt(HEAD)
    for item in range(2 * micro):
        spot = slice(item * length, (item + 1) * length)
        near = ctx_keep if item < micro else ctx_core
        inner = slice(item % micro * rows, (item % micro + 1) * rows)
        outer = slice(item * rows, (item + 1) * rows)
        for pair in range(quarter // 128):
            lanes = slice(pair * 128, (pair + 1) * 128)
            incoming = jnp.concatenate([near[inner, lanes], ctx_seq[outer, lanes]], axis=0)
            results = [[], [], []]
            for side in range(2):
                queries, keys, values = heads_of(qkv, spot, 2 * pair + side, quarter)
                probs = softmax(queries, keys, scale)
                own = incoming[:, side * HEAD : (side + 1) * HEAD]
                grad_probs = times_back(own, values)
                along = jnp.sum(probs * grad_probs, axis=-1, keepdims=True)
                grad_scores = (probs * (grad_probs - along)).astype(SHORT)
                results[0].append(times(grad_scores, keys) * scale)
                results[1].append(inner_rows(grad_scores, queries) * scale)
                results[2].append(inner_rows(probs.astype(SHORT), own))
            for third in range(3):
                start = third * quarter + pair * 128
                grad[spot, start : start + 128] = jnp.concatenate(results[third], axis=1).astype(
                    SHORT
                )
    line = column_sum(grad[...].astype(WIDE))
    vectors[...] = jnp.zeros_like(vectors)
    vectors[0:1, block(2 * half + core, quarter)] = line[:, :quarter]
    vectors[1:2, block(2 * half + core, quarter)] = line[:, 2 * quarter :]
    vectors[2:5, :] = sums_one[0:3, :]
    vectors[5:8, :] = sums_two[0:3, :]
    vectors[8:9, :] = up_sums[...]
    for step in range(PARTS):
        spot = block(where(step, chip), 128)
        chunks[step, :128, : 3 * quarter] = inner_rows(tokens[:, spot], grad[...]).astype(SHORT)
        chunks[step, :128, 3 * quarter :] = (
            out_keep[spot, :] + out_core[spot, :].astype(WIDE)
        ).astype(SHORT)
        lines = vectors[:, spot].astype(SHORT)
        chunks[step, 128:, :] = jnp.zeros((LINES, chunks.shape[2]), SHORT)
        chunks[step, 128:, :64] = lines[:, :64]
        chunks[step, 128:, LANES : LANES + 64] = lines[:, 64:]
        chunks[step, 128:, 2 * LANES : 2 * LANES + 128] = lines
    tall = tokens.shape[0] // 2
    for side in range(2):
        out = times_back(grad[side * tall : (side + 1) * tall, :], full[...])
        split_rows(out, side * tall, micro, rows, keep, send)


def build(mesh):
    devices = mesh.shape["dp"]
    chips = devices // CORES
    ringed = chips == PARTS
    half_ring = chips // 2
    ring = [2 * i for i in range(half_ring)] + [2 * i + 1 for i in reversed(range(half_ring))]
    same_core = [list(range(core, devices, CORES)) for core in range(CORES)]
    core_pairs = [(i, i ^ 1) for i in range(devices)]

    def hop(step):
        return [
            (ring[i] * CORES + core, ring[(i + step) % chips] * CORES + core)
            for i in range(chips)
            for core in range(CORES)
        ]

    onward, backward = hop(1), hop(-1)

    def swap_core(array):
        return lax.ppermute(array, "dp", core_pairs)

    def swap_seq(array):
        return lax.ppermute(array, "seq", [(0, 1), (1, 0)])

    def gather_ring(chunk, flip):
        far, near = (backward, onward) if flip else (onward, backward)
        got = [chunk]
        one = two = chunk
        for step in range(1, chips // 2 + 1):
            one = lax.ppermute(one, "dp", far)
            got.append(one)
            if step < chips // 2:
                two = lax.ppermute(two, "dp", near)
                got.append(two)
        return got

    def sum_ring(parts, flip):
        far, near = (onward, backward) if flip else (backward, onward)

        def run(perm, steps):
            moving = parts[steps[0]]
            for step in steps[1:]:
                moving = lax.ppermute(moving, "dp", perm)
                moving = (moving.astype(WIDE) + parts[step].astype(WIDE)).astype(SHORT)
            return lax.ppermute(moving, "dp", perm).astype(WIDE)

        long = list(range(chips - 1, 0, -2))
        short = list(range(chips - 2, 0, -2))
        return run(far, long) + run(near, short) + parts[0].astype(WIDE)

    def where(flip, step, chip):
        return part_index(step, flip, ringed, chip, chips)

    where_one = functools.partial(where, False)
    where_two = functools.partial(where, True)

    def per_device(
        inputs,
        cotangent,
        w_qkv,
        w_out,
        w_up,
        w_down,
        bias_q,
        bias_v,
        bias_out,
        gain_one,
        shift_one,
        bias_up,
        bias_down,
        gain_two,
        shift_two,
    ):
        index = lax.axis_index("dp")
        core = index % CORES
        half = lax.axis_index("seq")
        micro, rows, width = inputs.shape
        own_rows = micro * rows
        group = 4 * own_rows
        depth = w_qkv.shape[0]
        units = w_down.shape[0]
        tall = w_up.shape[1]
        quarter = width // 4
        side = 3 * quarter + width // 2
        several = chips // PARTS

        def share(own):
            from_seq = swap_seq(own)
            return own, from_seq, swap_core(own), swap_core(from_seq)

        def finish_sum(keep, from_core):
            moving = (keep[1] + from_core[1].astype(WIDE)).astype(SHORT)
            return swap_seq(moving)

        vectors = (
            bias_q,
            bias_v,
            bias_out,
            gain_one,
            shift_one,
            bias_down,
            gain_two,
            shift_two,
            bias_up,
        )
        mine, theirs = call(pack_kernel, [((depth + LINES, side), SHORT)] * 2, moved=10**6)(
            *[vector.reshape(1, -1) for vector in vectors], w_qkv, w_out
        )
        theirs = swap_core(theirs)
        square = in_order(core, mine[:depth], theirs[:depth], 0).reshape(2 * depth, side)
        lines = in_order(core, mine[depth:, :LANES], theirs[depth:, :LANES], 1)
        lines = jnp.pad(lines.reshape(LINES, 2 * LANES), ((0, 0), (0, side - 2 * LANES)))
        chunk_one = jnp.concatenate([square, lines], axis=0)

        by_unit = w_up.reshape(depth, chips, 2, 2, units // 2)
        by_unit = pick(by_unit, half, 3)
        mine = pick(by_unit, core, 2).reshape(depth, tall // 4)
        theirs = pick(by_unit, 1 - core, 2).reshape(depth, tall // 4)
        both = in_order(core, mine, swap_core(theirs), 0).reshape(2 * depth, tall // 4)
        own_down = pick(w_down.reshape(2, units // 2, width), half, 0)
        chunk_two = jnp.concatenate([both, own_down], axis=0)

        if ringed:
            chunks_one = gather_ring(chunk_one, False)
            chunk_two, _ = lax.optimization_barrier((chunk_two, chunks_one[5]))
            chunks_two = gather_ring(chunk_two, True)
        else:
            whole = lax.all_gather(chunk_one, "dp", axis_index_groups=same_core)
            square = whole[:, : 2 * depth].reshape(PARTS, 128, side)
            lines = whole[:, 2 * depth :, : 2 * LANES].reshape(chips, LINES, 2, LANES)
            slim = lines[:, :8, :, :depth].reshape(PARTS, several, 8, 2 * depth)
            slim = slim.transpose(0, 2, 1, 3).reshape(PARTS, 8, 2, 64)
            slim = jnp.pad(slim, ((0, 0), (0, 0), (0, 0), (0, LANES - 64)))
            slim = slim.reshape(PARTS, 8, 2 * LANES)
            bias = pick(lines[:, 8, :, :units], core, 1).reshape(chips, 2, units // 2)
            bias = pick(bias, half, 1).reshape(PARTS, 1, 128)
            lines = jnp.concatenate([slim, jnp.tile(bias, (1, 1, 2 * LANES // 128))], axis=1)
            lines = jnp.pad(lines, ((0, 0), (0, LINES - 9), (0, side - 2 * LANES)))
            whole = jnp.concatenate([square, lines], axis=1)
            chunks_one = [whole[step] for step in range(PARTS)]
            whole = lax.all_gather(chunk_two, "dp", axis_index_groups=same_core)
            whole = jnp.concatenate(
                [
                    whole[:, : 2 * depth].reshape(PARTS, 128, width),
                    whole[:, 2 * depth :].reshape(PARTS, 128, width),
                ],
                axis=1,
            )
            chunks_two = [whole[step] for step in range(PARTS)]

        flat = inputs.reshape(own_rows, width)
        tokens, full_qkv, qkv, ctx_keep, ctx_send, table, up_bias, out_mine = call(
            functools.partial(attention_kernel, micro, where_one),
            [
                ((group, width), SHORT),
                ((width, 3 * quarter), SHORT),
                ((group, 3 * quarter), SHORT),
                ((group // 2, quarter), SHORT),
                ((group // 2, quarter), SHORT),
                ((LINES, width), WIDE),
                ((1, tall // 4), WIDE),
                ((width, width // 2), SHORT),
            ],
            [((group, 3 * quarter), WIDE)],
            flops=2 * group * width * width,
            moved=8 * 10**6,
        )(*share(flat), *chunks_one)
        out_other = swap_core(out_mine)
        ctx_seq = swap_seq(ctx_send)
        ctx_core = swap_core(
            jnp.concatenate([ctx_keep[own_rows:], ctx_seq[own_rows:]], axis=1)
        )
        resid, first, first_low, context = call(
            first_kernel,
            [
                ((own_rows, width), WIDE),
                ((own_rows, width), WIDE),
                ((own_rows, width), SHORT),
                ((own_rows, width), SHORT),
            ],
            flops=2 * own_rows * width * width,
            moved=4 * 10**6,
        )(flat, ctx_keep, ctx_seq, ctx_core, out_mine, out_other, table)

        split_out = [((2, own_rows, width), WIDE), ((2, own_rows, width), SHORT)]
        first_group, full_up, full_down, pre_act, act, keep, send = call(
            functools.partial(forward_kernel, micro, where_two),
            [
                ((group, width), SHORT),
                ((width, tall // 4), SHORT),
                ((tall // 4, width), SHORT),
                ((group, tall // 4), WIDE),
                ((group, tall // 4), SHORT),
            ]
            + split_out,
            flops=group * width * tall,
            moved=16 * 10**6,
        )(*share(first_low), *chunks_two, up_bias)
        from_core = swap_core(send)
        from_seq = finish_sum(keep, from_core)
        layer_out, grad_two, mlp_low, sums_two = call(
            second_kernel,
            [
                ((own_rows, width), SHORT),
                ((own_rows, width), WIDE),
                ((own_rows, width), SHORT),
                ((8, width), WIDE),
            ],
            moved=3 * 10**6,
        )(first, keep, from_core, from_seq, table, cotangent.reshape(own_rows, width))

        grads_two, keep, send, up_sums = call(
            functools.partial(backward_kernel, micro, where_two),
            [((PARTS, 256, width), SHORT)] + split_out + [((1, tall // 4), WIDE)],
            [((group, width), SHORT), ((group, tall // 4), SHORT)],
            flops=2 * group * width * tall,
            moved=16 * 10**6,
        )(*share(mlp_low), first_group, full_up, full_down, pre_act, act)
        from_core = swap_core(send)
        from_seq = finish_sum(keep, from_core)
        grad_one, out_keep, out_send, grad_keep, grad_send, sums_one = call(
            first_back_kernel,
            [
                ((own_rows, width), WIDE),
                ((width, width // 2), WIDE),
                ((width, width // 2), SHORT),
                ((own_rows, width // 2), SHORT),
                ((own_rows, width // 2), SHORT),
                ((8, width), WIDE),
            ],
            flops=4 * own_rows * width * width,
            moved=8 * 10**6,
        )(resid, grad_two, keep, from_core, from_seq, table, context, out_mine, out_other)
        grad_core = swap_core(grad_send)
        grad_seq = swap_seq(jnp.concatenate([grad_keep[:, quarter:], grad_core[:, quarter:]]))
        out_core = swap_core(out_send)
        grads_one, keep, send = call(
            functools.partial(attention_back_kernel, micro, where_one),
            [((PARTS, 128 + LINES, side), SHORT)] + split_out,
            [((group, 3 * quarter), SHORT), ((LINES, width), WIDE)],
            flops=3 * group * width * width,
            moved=12 * 10**6,
        )(
            qkv,
            grad_keep,
            grad_core,
            grad_seq,
            tokens,
            full_qkv,
            out_keep,
            out_core,
            sums_two,
            sums_one,
            up_sums,
        )
        from_core = swap_core(send)
        from_seq = finish_sum(keep, from_core)
        input_grad = grad_one + (keep[0] + from_core[0].astype(WIDE) + from_seq.astype(WIDE))

        if ringed:
            share_two = sum_ring(grads_two, True)
            share_one = sum_ring(grads_one, False)
        else:
            whole = jnp.concatenate(
                [
                    grads_two[:, :128].reshape(chips, 2 * depth, width),
                    grads_two[:, 128:].reshape(chips, units // 2, width),
                ],
                axis=1,
            )
            share_two = lax.psum_scatter(whole, "dp", axis_index_groups=same_core).astype(WIDE)
            square = grads_one[:, :128].reshape(chips, 2 * depth, side)
            slim = grads_one[:, 128 : 128 + 8, : 2 * LANES].reshape(PARTS, 8, 2, LANES)[..., :64]
            slim = slim.reshape(PARTS, 8, several, 2 * depth).transpose(0, 2, 1, 3)
            slim = slim.reshape(chips, 8, 2, depth)
            slim = jnp.pad(slim, ((0, 0), (0, LINES - 8), (0, 0), (0, LANES - depth)))
            bias = grads_one[:, 128 + 8, 2 * LANES : 2 * LANES + 128]
            bias = bias.reshape(chips, 1, units // 2)
            bias = jnp.pad(
                bias, ((0, 0), (8, LINES - 9), (0, side - 2 * LANES - units // 2))
            )
            lines = jnp.concatenate([slim.reshape(chips, LINES, 2 * LANES), bias], axis=2)
            whole = jnp.concatenate([square, lines], axis=1)
            share_one = lax.psum_scatter(whole, "dp", axis_index_groups=same_core).astype(WIDE)

        split = share_two[: 2 * depth].reshape(2, depth, width).astype(SHORT)
        own, other = pick(split, core, 0), swap_core(pick(split, 1 - core, 0))
        own_down = share_two[2 * depth :].astype(SHORT)
        moved = swap_seq(jnp.concatenate([own, other, own_down], axis=0))
        by_chip = (depth, chips, units // 2)
        near = in_order(core, own.reshape(by_chip), other.reshape(by_chip), 2)
        away = in_order(
            core, moved[:depth].reshape(by_chip), moved[depth : 2 * depth].reshape(by_chip), 2
        )
        final_up = in_order(half, near, away, 3).reshape(depth, tall).astype(WIDE)
        final_down = in_order(half, own_down, moved[2 * depth :], 0)
        final_down = final_down.reshape(units, width).astype(WIDE)

        split = share_one[: 2 * depth].reshape(2, depth, side).astype(SHORT)
        lines = share_one[2 * depth :, : 2 * LANES].reshape(LINES, 2, LANES)
        packet = jnp.pad(pick(lines, 1 - core, 1).astype(SHORT), ((0, 0), (0, side - LANES)))
        other = swap_core(jnp.concatenate([pick(split, 1 - core, 0), packet], axis=0))
        own = pick(split, core, 0)
        line = pick(lines, core, 1) + other[depth:, :LANES].astype(WIDE)
        bias = share_one[2 * depth + 8, 2 * LANES : 2 * LANES + units // 2]
        packet = jnp.concatenate(
            [line.astype(SHORT), share_one[2 * depth :, 2 * LANES :].astype(SHORT)], axis=1
        )
        packet = jnp.pad(packet, ((0, 0), (0, LANES)))
        moved = swap_seq(jnp.concatenate([own, other[:depth], packet], axis=0))
        by_third = (depth, 3, quarter)
        near = in_order(
            core,
            own[:, : 3 * quarter].reshape(by_third),
            other[:depth, : 3 * quarter].reshape(by_third),
            2,
        )
        away = in_order(
            core,
            moved[:depth, : 3 * quarter].reshape(by_third),
            moved[depth : 2 * depth, : 3 * quarter].reshape(by_third),
            2,
        )
        final_qkv = in_order(half, near, away, 2).reshape(depth, 3 * width).astype(WIDE)
        near = own[:, 3 * quarter :].astype(WIDE) + moved[:depth, 3 * quarter :].astype(WIDE)
        away = other[:depth, 3 * quarter :].astype(WIDE) + moved[
            depth : 2 * depth, 3 * quarter :
        ].astype(WIDE)
        final_out = in_order(core, near, away, 1).reshape(depth, width)
        line = line + moved[2 * depth :, :LANES].astype(WIDE)
        finals = [line[i, :depth] for i in range(8)]
        from_seq = moved[2 * depth + 8, LANES : LANES + units // 2].astype(WIDE)
        final_bias = in_order(half, bias, from_seq, 0).reshape(-1)

        return (
            layer_out.reshape(inputs.shape),
            input_grad.reshape(inputs.shape),
            final_qkv,
            final_out,
            final_up,
            final_down,
            finals[0],
            finals[1],
            finals[2],
            finals[3],
            finals[4],
            final_bias,
            finals[5],
            finals[6],
            finals[7],
        )

    return per_device


def solution(mesh):
    token = P(None, ("dp", "seq"), None)
    matrix = P("dp", None)
    vector = P("dp")
    placed = (token, token) + (matrix,) * 4 + (vector,) * 9
    return jax.shard_map(
        build(mesh), mesh=mesh, in_specs=placed, out_specs=placed, check_vma=False
    )
```

```python
import functools
import math

import jax
import jax.numpy as jnp
from jax import lax
from jax.experimental import pallas as pl
from jax.experimental.pallas import tpu as pltpu
from jax.sharding import PartitionSpec as P

HEAD = 64
CORES = 2
PARTS = 8
SHORT = jnp.bfloat16
WIDE = jnp.float32
LIMIT = 24 * 1024 * 1024
WHOLE = 56 * 1024 * 1024
LINES = 16
LANES = 256


def gelu_exact(values):
    return 0.5 * values * (1.0 + lax.erf(values * (1.0 / math.sqrt(2.0))))


def gelu_slope(values):
    bell = jnp.exp(values * values * -0.5) * (1.0 / math.sqrt(2.0 * math.pi))
    return 0.5 * (1.0 + lax.erf(values * (1.0 / math.sqrt(2.0)))) + values * bell


def times(left, right):
    return jnp.dot(left, right, preferred_element_type=WIDE)


def times_back(left, right):
    return lax.dot_general(left, right, (((1,), (1,)), ((), ())), preferred_element_type=WIDE)


def inner_rows(left, right):
    return lax.dot_general(left, right, (((0,), (0,)), ((), ())), preferred_element_type=WIDE)


def column_sum(part):
    return jnp.sum(part, axis=0, keepdims=True)


def standard(features):
    centre = jnp.mean(features, axis=-1, keepdims=True)
    centred = features - centre
    spread = jnp.mean(centred * centred, axis=-1, keepdims=True)
    slope = lax.rsqrt(spread + 1e-12)
    return centred * slope, slope


def standard_back(normal, slope, grad):
    even = jnp.mean(grad, axis=-1, keepdims=True)
    along = jnp.mean(normal * grad, axis=-1, keepdims=True)
    return slope * (grad - even - normal * along)


def pick(array, index, axis):
    return lax.dynamic_index_in_dim(array, index, axis, keepdims=False)


def in_order(place, own, other, axis):
    first = place == 0
    return jnp.stack([jnp.where(first, own, other), jnp.where(first, other, own)], axis=axis)


def block(index, size):
    return pl.ds(pl.multiple_of(index * size, size), size)


def here():
    index = lax.axis_index("dp")
    return lax.div(index, CORES), lax.rem(index, CORES), lax.axis_index("seq")


def part_index(step, flip, ringed, chip, chips):
    if not ringed:
        return step
    half = chips // 2
    upper = lax.rem(chip, 2)
    level = lax.div(chip, 2)
    spot = jnp.where(upper == 0, level, chips - 1 - level)
    away = (step + 1) // 2
    sign = -1 if (step % 2 == 1) != flip else 1
    spot = lax.rem(spot + sign * away + chips, chips)
    return jnp.where(spot < half, 2 * spot, 2 * (chips - 1 - spot) + 1)


def call(body, outs, scratch=(), flops=0, moved=0, limit=LIMIT):
    return pl.pallas_call(
        body,
        out_shape=[jax.ShapeDtypeStruct(shape, kind) for shape, kind in outs],
        scratch_shapes=[pltpu.VMEM(shape, kind) for shape, kind in scratch],
        compiler_params=pltpu.CompilerParams(vmem_limit_bytes=limit),
        cost_estimate=pl.CostEstimate(flops=flops, bytes_accessed=moved, transcendentals=0),
    )


def pack_kernel(*refs):
    vectors, up_bias, w_qkv, w_out, mine, theirs = refs[:8], *refs[8:]
    _, core, half = here()
    depth = w_qkv.shape[0]
    width = w_out.shape[1]
    quarter = width // 4
    for out, which in ((mine, core), (theirs, 1 - core)):
        for third in range(3):
            start = third * width + (2 * half + which) * quarter
            out[:depth, third * quarter : (third + 1) * quarter] = w_qkv[
                :, pl.ds(pl.multiple_of(start, quarter), quarter)
            ]
        out[:depth, 3 * quarter :] = w_out[:, block(which, width // 2)]
        lines = [
            jnp.pad(vector[...], ((0, 0), (0, LANES - depth))).astype(WIDE) for vector in vectors
        ]
        lines.append(jnp.pad(up_bias[...].astype(WIDE), ((0, 0), (0, LANES - up_bias.shape[1]))))
        lines.append(jnp.zeros((LINES - 9, LANES), WIDE))
        out[depth:, :LANES] = jnp.concatenate(lines, axis=0).astype(SHORT)
        out[depth:, LANES:] = jnp.zeros((LINES, out.shape[1] - LANES), SHORT)


def heads_of(qkv, rows, head, quarter):
    return [
        qkv[rows, third * quarter + head * HEAD : third * quarter + (head + 1) * HEAD]
        for third in range(3)
    ]


def softmax(queries, keys, scale):
    scores = times_back(queries, keys) * scale
    expo = jnp.exp(scores - jnp.max(scores, axis=-1, keepdims=True))
    return expo / jnp.sum(expo, axis=-1, keepdims=True)


def fill_group(group, pieces, micro):
    rows = pieces[0].shape[0] // micro
    for place in range(4 * micro):
        far, item, side = place // (2 * micro), place // 2 % micro, place % 2
        group[place * rows : (place + 1) * rows, :] = pieces[2 * far + side][
            item * rows : (item + 1) * rows, :
        ]


def attention_kernel(micro, where, *refs):
    pieces, chunks, rest = refs[:4], refs[4:13], refs[13:]
    tokens, full, qkv, keep, send, kept, vectors, up_bias, out_half, wide = rest
    chip, core, half = here()
    quarter = keep.shape[1]
    scale = 1.0 / math.sqrt(HEAD)
    fill_group(tokens, pieces, micro)
    for step in range(PARTS):
        spot = block(where(step, chip), 128)
        chunk, start = chunks[step], 128
        if step < PARTS - 1:
            full[spot, :] = chunk[:128, : 3 * quarter]
            out_half[spot, :] = chunk[:128, 3 * quarter :]
        else:
            for side in range(2):
                piece = chunks[step + side]
                inner = block(2 * where(step, chip) + side, 64)
                full[inner, :] = piece[:64, : 3 * quarter]
                out_half[inner, :] = piece[:64, 3 * quarter :]
            chunk, start = piece, 64
        lines = jnp.concatenate([chunk[start:, :64], chunk[start:, LANES : LANES + 64]], axis=1)
        vectors[:, spot] = lines.astype(WIDE)
        lines = chunk[start:, block(core * (LANES // 128) + half, 128)]
        up_bias[:, spot] = lines.astype(WIDE)[8:9, :]
    wide[...] = times(tokens[...], full[...])
    spot = block(2 * half + core, quarter)
    qkv[:, :quarter] = (wide[:, :quarter] + vectors[0:1, spot]).astype(SHORT)
    qkv[:, quarter : 2 * quarter] = wide[:, quarter : 2 * quarter].astype(SHORT)
    qkv[:, 2 * quarter :] = (wide[:, 2 * quarter :] + vectors[1:2, spot]).astype(SHORT)
    length = tokens.shape[0] // (2 * micro)
    rows = length // 2
    for item in range(2 * micro):
        for pair in range(quarter // 128):
            both = []
            for head in (2 * pair, 2 * pair + 1):
                queries, keys, values = heads_of(
                    qkv, slice(item * length, (item + 1) * length), head, quarter
                )
                probs = softmax(queries, keys, scale)
                kept[item * (quarter // HEAD) + head] = probs
                both.append(times(probs.astype(SHORT), values))
            both = jnp.concatenate(both, axis=1).astype(SHORT)
            spot = slice(pair * 128, (pair + 1) * 128)
            keep[item * rows : (item + 1) * rows, spot] = both[:rows]
            send[item * rows : (item + 1) * rows, spot] = both[rows:]


def first_kernel(
    inputs, keep, from_seq, from_core, mine, other, vectors, resid, first, low, context
):
    _, core, half = here()
    rows, width = inputs.shape
    quarter = width // 4
    flip_core, flip_half = 1 - core, 1 - half
    context[:, block(2 * half + core, quarter)] = keep[:rows, :]
    context[:, block(2 * flip_half + core, quarter)] = from_seq[:rows, :]
    context[:, block(2 * half + flip_core, quarter)] = from_core[:, :quarter]
    context[:, block(2 * flip_half + flip_core, quarter)] = from_core[:, quarter:]
    whole = context[...]
    resid[:, block(core, width // 2)] = times(whole, mine[...])
    resid[:, block(flip_core, width // 2)] = times(whole, other[...])
    features = inputs[...].astype(WIDE) + (resid[...] + vectors[2:3, :])
    resid[...] = features
    normal, _ = standard(features)
    features = normal * vectors[3:4, :] + vectors[4:5, :]
    first[...] = features
    low[...] = features.astype(SHORT)


def split_rows(value, start, micro, rows, keep, send):
    for place in range(value.shape[0] // rows):
        far, item, side = (
            (start + place * rows) // rows // (2 * micro),
            (start + place * rows) // rows // 2 % micro,
            (start + place * rows) // rows % 2,
        )
        part = value[place * rows : (place + 1) * rows, :]
        if far:
            send[side, item * rows : (item + 1) * rows, :] = part.astype(SHORT)
        else:
            keep[side, item * rows : (item + 1) * rows, :] = part


def forward_kernel(micro, where, *refs):
    pieces, chunks, up_bias, rest = refs[:4], refs[4:22], refs[22], refs[23:]
    group, full_up, full_down, pre_act, act, keep, send = rest
    chip, _, _ = here()
    fill_group(group, pieces, micro)
    for full, parts in ((full_up, chunks[:9]), (full_down, chunks[9:])):
        for step in range(PARTS - 1):
            full[block(where(step, chip), 128), :] = parts[step][...]
        for side in range(2):
            full[block(2 * where(PARTS - 1, chip) + side, 64), :] = parts[PARTS - 1 + side][...]
    rows = pieces[0].shape[0] // micro
    tall = group.shape[0] // 2
    for side in range(2):
        spot = slice(side * tall, (side + 1) * tall)
        pre = times(group[spot, :], full_up[...]) + up_bias[...]
        pre_act[spot, :] = pre
        act[spot, :] = gelu_exact(pre).astype(SHORT)
        out = times(act[spot, :], full_down[...])
        split_rows(out, side * tall, micro, rows, keep, send)


def slope_kernel(pre_act, slope):
    for start in range(0, pre_act.shape[0], 64):
        slope[start : start + 64, :] = gelu_slope(pre_act[start : start + 64, :])


def second_kernel(
    first, keep, from_core, from_seq, vectors, cotangent, out, grad, low, sums
):
    mlp = keep[0] + from_core[0].astype(WIDE) + from_seq[...].astype(WIDE)
    normal, slope = standard(first[...] + (mlp + vectors[5:6, :]))
    out[...] = (normal * vectors[6:7, :] + vectors[7:8, :]).astype(SHORT)
    incoming = cotangent[...].astype(WIDE)
    resid = standard_back(normal, slope, incoming * vectors[6:7, :])
    grad[...] = resid
    short = resid.astype(SHORT)
    low[...] = short
    sums[...] = jnp.zeros_like(sums)
    sums[0:1, :] = column_sum(short.astype(WIDE))
    sums[1:2, :] = column_sum(incoming * normal)
    sums[2:3, :] = column_sum(incoming)


def backward_kernel(micro, where, *refs):
    pieces, rest = refs[:4], refs[4:]
    group, full_up, full_down, slopes, act, chunks_up, chunks_down, keep, send, sums, grad, pre = rest
    chip, _, _ = here()
    fill_group(grad, pieces, micro)
    rows = pieces[0].shape[0] // micro
    tall = grad.shape[0] // 2
    total = None
    for side in range(2):
        spot = slice(side * tall, (side + 1) * tall)
        part = (times_back(grad[spot, :], full_down[...]) * slopes[spot, :]).astype(SHORT)
        pre[spot, :] = part
        part = column_sum(part.astype(WIDE))
        total = part if total is None else total + part
    sums[...] = total
    for step in range(PARTS):
        spot = block(where(step, chip), 128)
        chunks_down[step] = inner_rows(act[:, spot], grad[...]).astype(SHORT)
        chunks_up[step] = inner_rows(group[:, spot], pre[...]).astype(SHORT)
    for side in range(2):
        spot = slice(side * tall, (side + 1) * tall)
        out = times_back(pre[spot, :], full_up[...])
        split_rows(out, side * tall, micro, rows, keep, send)


def first_back_kernel(
    resid,
    grad_two,
    keep,
    from_core,
    from_seq,
    vectors,
    context,
    mine,
    other,
    grad,
    out_keep,
    out_send,
    ctx_keep,
    ctx_send,
    sums,
):
    _, core, half = here()
    width = resid.shape[1]
    quarter = width // 4
    incoming = grad_two[...] + (keep[0] + from_core[0].astype(WIDE) + from_seq[...].astype(WIDE))
    normal, slope = standard(resid[...])
    value = standard_back(normal, slope, incoming * vectors[3:4, :])
    grad[...] = value
    short = value.astype(SHORT)
    sums[...] = jnp.zeros_like(sums)
    sums[0:1, :] = column_sum(short.astype(WIDE))
    sums[1:2, :] = column_sum(incoming * normal)
    sums[2:3, :] = column_sum(incoming)
    left, right = short[:, : width // 2], short[:, width // 2 :]
    own = jnp.where(core == 0, left, right)
    away = jnp.where(core == 0, right, left)
    out_keep[...] = inner_rows(context[...], own)
    out_send[...] = inner_rows(context[...], away).astype(SHORT)
    for target, which in ((ctx_keep, core), (ctx_send, 1 - core)):
        for side, which_half in enumerate((half, 1 - half)):
            spot = block(2 * which_half + which, quarter)
            value = times_back(own, mine[spot, :]) + times_back(away, other[spot, :])
            target[:, side * quarter : (side + 1) * quarter] = value.astype(SHORT)


def attention_back_kernel(micro, where, *refs):
    qkv, kept, ctx_keep, ctx_core, ctx_seq, tokens, out_keep, out_core = refs[:8]
    sums_two, sums_one, up_sums, chunks, grad, flag, vectors = refs[8:]
    chip, core, half = here()
    quarter = qkv.shape[1] // 3
    length = qkv.shape[0] // (2 * micro)
    rows = length // 2
    scale = 1.0 / math.sqrt(HEAD)
    for item in range(2 * micro):
        spot = slice(item * length, (item + 1) * length)
        near = ctx_keep if item < micro else ctx_core
        inner = slice(item % micro * rows, (item % micro + 1) * rows)
        outer = slice(item * rows, (item + 1) * rows)
        for pair in range(quarter // 128):
            lanes = slice(pair * 128, (pair + 1) * 128)
            incoming = jnp.concatenate([near[inner, lanes], ctx_seq[outer, lanes]], axis=0)
            results = [[], [], []]
            for side in range(2):
                queries, keys, values = heads_of(qkv, spot, 2 * pair + side, quarter)
                probs = kept[item * (quarter // HEAD) + 2 * pair + side]
                own = incoming[:, side * HEAD : (side + 1) * HEAD]
                grad_probs = times_back(own, values)
                along = jnp.sum(probs * grad_probs, axis=-1, keepdims=True)
                grad_scores = (probs * (grad_probs - along)).astype(SHORT)
                results[0].append(times(grad_scores, keys) * scale)
                results[1].append(inner_rows(grad_scores, queries) * scale)
                results[2].append(inner_rows(probs.astype(SHORT), own))
            for third in range(3):
                start = third * quarter + pair * 128
                grad[spot, start : start + 128] = jnp.concatenate(results[third], axis=1).astype(
                    SHORT
                )
    line = column_sum(grad[...].astype(WIDE))
    vectors[...] = jnp.zeros_like(vectors)
    vectors[0:1, block(2 * half + core, quarter)] = line[:, :quarter]
    vectors[1:2, block(2 * half + core, quarter)] = line[:, 2 * quarter :]
    vectors[2:5, :] = sums_one[0:3, :]
    vectors[5:8, :] = sums_two[0:3, :]
    vectors[8:9, :] = up_sums[...]
    flag[...] = vectors[0:8, 0:128]
    for step in range(PARTS):
        spot = block(where(step, chip), 128)
        chunks[step, :128, : 3 * quarter] = inner_rows(tokens[:, spot], grad[...]).astype(SHORT)
        chunks[step, :128, 3 * quarter :] = (
            out_keep[spot, :] + out_core[spot, :].astype(WIDE)
        ).astype(SHORT)
        lines = vectors[:, spot].astype(SHORT)
        chunks[step, 128:, :] = jnp.zeros((LINES, chunks.shape[2]), SHORT)
        chunks[step, 128:, :64] = lines[:, :64]
        chunks[step, 128:, LANES : LANES + 64] = lines[:, 64:]
        chunks[step, 128:, 2 * LANES : 2 * LANES + 128] = lines


def input_back_kernel(micro, rows, grad, full, keep, send):
    tall = grad.shape[0] // 2
    for side in range(2):
        out = times_back(grad[side * tall : (side + 1) * tall, :], full[...])
        split_rows(out, side * tall, micro, rows, keep, send)


def after(gate, *values):
    if gate is None:
        return values
    return lax.optimization_barrier((*values, gate))[:-1]


def build(mesh):
    devices = mesh.shape["dp"]
    chips = devices // CORES
    ringed = chips == PARTS
    half_ring = chips // 2
    ring = [2 * i for i in range(half_ring)] + [2 * i + 1 for i in reversed(range(half_ring))]
    same_core = [list(range(core, devices, CORES)) for core in range(CORES)]
    core_pairs = [(i, i ^ 1) for i in range(devices)]

    def hop(step):
        return [
            (ring[i] * CORES + core, ring[(i + step) % chips] * CORES + core)
            for i in range(chips)
            for core in range(CORES)
        ]

    onward, backward = hop(1), hop(-1)

    def swap_core(array):
        return lax.ppermute(array, "dp", core_pairs)

    def swap_seq(array):
        return lax.ppermute(array, "seq", [(0, 1), (1, 0)])

    def gather_ring(chunk, cut, flip, gates=(None, None, None)):
        far, near = (backward, onward) if flip else (onward, backward)
        got = [chunk]
        one = two = chunk
        for step in range(chips // 2 - 1):
            if step:
                one, two = after(gates[step - 1], one, two)
            one = lax.ppermute(one, "dp", far)
            two = lax.ppermute(two, "dp", near)
            got += [one, two]
        one, two = after(gates[-1], one, two)
        return got + [lax.ppermute(one[:cut], "dp", far), lax.ppermute(two[cut:], "dp", near)]

    def sum_ring(parts, cut, flip, gates=(None, None, None)):
        far, near = (onward, backward) if flip else (backward, onward)
        last = parts[chips - 1]
        one, two = last[:cut], last[cut:]
        for step in range(chips // 2 - 1):
            one = lax.ppermute(one, "dp", far)
            two = lax.ppermute(two, "dp", near)
            one, two = after(gates[step], one, two)
            one, two = one.astype(WIDE), two.astype(WIDE)
            place = chips - 3 - 2 * step
            here, there = parts[place].astype(WIDE), parts[place + 1].astype(WIDE)
            if step:
                one, two = one + here, two + there
            else:
                one = jnp.concatenate([one + here[:cut], here[cut:]], axis=0)
                two = jnp.concatenate([there[:cut], two + there[cut:]], axis=0)
            one, two = one.astype(SHORT), two.astype(SHORT)
        one = lax.ppermute(one, "dp", far)
        two = lax.ppermute(two, "dp", near)
        return one.astype(WIDE) + two.astype(WIDE) + parts[0].astype(WIDE)

    def where(flip, step, chip):
        return part_index(step, flip, ringed, chip, chips)

    where_one = functools.partial(where, False)
    where_two = functools.partial(where, True)

    def per_device(
        inputs,
        cotangent,
        w_qkv,
        w_out,
        w_up,
        w_down,
        bias_q,
        bias_v,
        bias_out,
        gain_one,
        shift_one,
        bias_up,
        bias_down,
        gain_two,
        shift_two,
    ):
        index = lax.axis_index("dp")
        core = index % CORES
        half = lax.axis_index("seq")
        micro, rows, width = inputs.shape
        own_rows = micro * rows
        group = 4 * own_rows
        depth = w_qkv.shape[0]
        units = w_down.shape[0]
        tall = w_up.shape[1]
        quarter = width // 4
        side = 3 * quarter + width // 2
        several = chips // PARTS

        def share(own):
            from_seq = swap_seq(own)
            return own, from_seq, swap_core(own), swap_core(from_seq)

        def finish_sum(keep, from_core):
            moving = (keep[1] + from_core[1].astype(WIDE)).astype(SHORT)
            return swap_seq(moving)

        vectors = (
            bias_q,
            bias_v,
            bias_out,
            gain_one,
            shift_one,
            bias_down,
            gain_two,
            shift_two,
            bias_up,
        )
        mine, theirs = call(pack_kernel, [((depth + LINES, side), SHORT)] * 2, moved=10**6, limit=WHOLE)(
            *[vector.reshape(1, -1) for vector in vectors], w_qkv, w_out
        )
        theirs = swap_core(theirs)
        square = in_order(core, mine[:depth], theirs[:depth], 0).reshape(2 * depth, side)
        lines = in_order(core, mine[depth:, :LANES], theirs[depth:, :LANES], 1)
        lines = jnp.pad(lines.reshape(LINES, 2 * LANES), ((0, 0), (0, side - 2 * LANES)))
        chunk_one = jnp.concatenate([square, lines], axis=0)

        by_unit = w_up.reshape(depth, chips, 2, 2, units // 2)
        by_unit = pick(by_unit, half, 3)
        mine = pick(by_unit, core, 2).reshape(depth, tall // 4)
        theirs = pick(by_unit, 1 - core, 2).reshape(depth, tall // 4)
        both = in_order(core, mine, swap_core(theirs), 0).reshape(2 * depth, tall // 4)
        own_down = pick(w_down.reshape(2, units // 2, width), half, 0)
        chunk_two, chunk_three = both, own_down

        flat = inputs.reshape(own_rows, width)
        shared = share(flat)
        if ringed:
            chunks_one = gather_ring(chunk_one, 64, False, (chunk_two, shared[1], None))
            chunk_two, chunk_three = after(chunks_one[5], chunk_two, chunk_three)
        else:
            whole = lax.all_gather(chunk_one, "dp", axis_index_groups=same_core)
            square = whole[:, : 2 * depth].reshape(PARTS, 128, side)
            lines = whole[:, 2 * depth :, : 2 * LANES].reshape(chips, LINES, 2, LANES)
            slim = lines[:, :8, :, :depth].reshape(PARTS, several, 8, 2 * depth)
            slim = slim.transpose(0, 2, 1, 3).reshape(PARTS, 8, 2, 64)
            slim = jnp.pad(slim, ((0, 0), (0, 0), (0, 0), (0, LANES - 64)))
            slim = slim.reshape(PARTS, 8, 2 * LANES)
            bias = pick(lines[:, 8, :, :units], core, 1).reshape(chips, 2, units // 2)
            bias = pick(bias, half, 1).reshape(PARTS, 1, 128)
            lines = jnp.concatenate([slim, jnp.tile(bias, (1, 1, 2 * LANES // 128))], axis=1)
            lines = jnp.pad(lines, ((0, 0), (0, LINES - 9), (0, side - 2 * LANES)))
            whole = jnp.concatenate([square, lines], axis=1)
            chunks_one = [whole[step] for step in range(PARTS - 1)]
            chunks_one += [whole[-1, :64], whole[-1, 64:]]
            chunks_two = []
            for chunk in (chunk_two, chunk_three):
                whole = lax.all_gather(chunk, "dp", axis_index_groups=same_core)
                whole = whole.reshape(PARTS, 128, width)
                chunks_two += [whole[step] for step in range(PARTS - 1)]
                chunks_two += [whole[-1, :64], whole[-1, 64:]]

        tokens, full_qkv, qkv, ctx_keep, ctx_send, probs, table, up_bias, out_mine = call(
            functools.partial(attention_kernel, micro, where_one),
            [
                ((group, width), SHORT),
                ((width, 3 * quarter), SHORT),
                ((group, 3 * quarter), SHORT),
                ((group // 2, quarter), SHORT),
                ((group // 2, quarter), SHORT),
                ((2 * micro * quarter // HEAD, 2 * rows, 2 * rows), WIDE),
                ((LINES, width), WIDE),
                ((1, tall // 4), WIDE),
                ((width, width // 2), SHORT),
            ],
            [((group, 3 * quarter), WIDE)],
            flops=2 * group * width * width,
            moved=8 * 10**6,
        )(*shared, *chunks_one)
        out_other = swap_core(out_mine)
        ctx_seq = swap_seq(ctx_send)
        ctx_core = swap_core(
            jnp.concatenate([ctx_keep[own_rows:], ctx_seq[own_rows:]], axis=1)
        )
        resid, first, first_low, context = call(
            first_kernel,
            [
                ((own_rows, width), WIDE),
                ((own_rows, width), WIDE),
                ((own_rows, width), SHORT),
                ((own_rows, width), SHORT),
            ],
            flops=2 * own_rows * width * width,
            moved=4 * 10**6,
        )(flat, ctx_keep, ctx_seq, ctx_core, out_mine, out_other, table)

        pieces = share(first_low)
        if ringed:
            gates = (ctx_seq, pieces[1], None)
            chunks_two = gather_ring(chunk_two, 64, True, gates)
            chunks_two += gather_ring(chunk_three, 64, True, gates)
        split_out = [((2, own_rows, width), WIDE), ((2, own_rows, width), SHORT)]
        first_group, full_up, full_down, pre_act, act, keep, send = call(
            functools.partial(forward_kernel, micro, where_two),
            [
                ((group, width), SHORT),
                ((width, tall // 4), SHORT),
                ((tall // 4, width), SHORT),
                ((group, tall // 4), WIDE),
                ((group, tall // 4), SHORT),
            ]
            + split_out,
            flops=group * width * tall,
            moved=16 * 10**6,
        )(*pieces, *chunks_two, up_bias)
        from_core = swap_core(send)
        moving = (keep[1] + from_core[1].astype(WIDE)).astype(SHORT)
        (pre_act,) = after(moving, pre_act)
        (slopes,) = call(slope_kernel, [((group, tall // 4), WIDE)], moved=5 * 10**6)(pre_act)
        from_seq = swap_seq(moving)
        layer_out, grad_two, mlp_low, sums_two = call(
            second_kernel,
            [
                ((own_rows, width), SHORT),
                ((own_rows, width), WIDE),
                ((own_rows, width), SHORT),
                ((8, width), WIDE),
            ],
            moved=3 * 10**6,
        )(first, keep, from_core, from_seq, table, cotangent.reshape(own_rows, width))

        grads_two, grads_three, keep, send, up_sums = call(
            functools.partial(backward_kernel, micro, where_two),
            [((PARTS, 128, width), SHORT)] * 2 + split_out + [((1, tall // 4), WIDE)],
            [((group, width), SHORT), ((group, tall // 4), SHORT)],
            flops=2 * group * width * tall,
            moved=16 * 10**6,
        )(*share(mlp_low), first_group, full_up, full_down, slopes, act)
        from_core = swap_core(send)
        from_seq = finish_sum(keep, from_core)
        gate_one = from_seq
        grad_one, out_keep, out_send, grad_keep, grad_send, sums_one = call(
            first_back_kernel,
            [
                ((own_rows, width), WIDE),
                ((width, width // 2), WIDE),
                ((width, width // 2), SHORT),
                ((own_rows, width // 2), SHORT),
                ((own_rows, width // 2), SHORT),
                ((8, width), WIDE),
            ],
            flops=4 * own_rows * width * width,
            moved=8 * 10**6,
        )(resid, grad_two, keep, from_core, from_seq, table, context, out_mine, out_other)
        grad_core = swap_core(grad_send)
        grad_seq = swap_seq(jnp.concatenate([grad_keep[:, quarter:], grad_core[:, quarter:]]))
        out_core = swap_core(out_send)
        grads_one, grad_tokens, flag = call(
            functools.partial(attention_back_kernel, micro, where_one),
            [
                ((PARTS, 128 + LINES, side), SHORT),
                ((group, 3 * quarter), SHORT),
                ((8, 128), WIDE),
            ],
            [((LINES, width), WIDE)],
            flops=3 * group * width * width,
            moved=12 * 10**6,
        )(
            qkv,
            probs,
            grad_keep,
            grad_core,
            grad_seq,
            tokens,
            out_keep,
            out_core,
            sums_two,
            sums_one,
            up_sums,
        )
        keep, send = call(
            functools.partial(input_back_kernel, micro, rows),
            split_out,
            flops=group * width * width,
            moved=5 * 10**6,
        )(grad_tokens, full_qkv)
        from_core = swap_core(send)
        moving = (keep[1] + from_core[1].astype(WIDE)).astype(SHORT)
        from_seq = swap_seq(moving)
        gates_one = (moving, from_seq, None)
        input_grad = grad_one + (keep[0] + from_core[0].astype(WIDE) + from_seq.astype(WIDE))

        if ringed:
            share_three = sum_ring(grads_three, 64, True, (gate_one, flag, None))
            share_two = sum_ring(grads_two, 64, True, (gate_one, flag, None))
            share_one = sum_ring(grads_one, 64, False, gates_one)
        else:
            whole = grads_three.reshape(chips, units // 2, width)
            share_three = lax.psum_scatter(whole, "dp", axis_index_groups=same_core).astype(WIDE)
            whole = grads_two.reshape(chips, 2 * depth, width)
            share_two = lax.psum_scatter(whole, "dp", axis_index_groups=same_core).astype(WIDE)
            square = grads_one[:, :128].reshape(chips, 2 * depth, side)
            slim = grads_one[:, 128 : 128 + 8, : 2 * LANES].reshape(PARTS, 8, 2, LANES)[..., :64]
            slim = slim.reshape(PARTS, 8, several, 2 * depth).transpose(0, 2, 1, 3)
            slim = slim.reshape(chips, 8, 2, depth)
            slim = jnp.pad(slim, ((0, 0), (0, LINES - 8), (0, 0), (0, LANES - depth)))
            bias = grads_one[:, 128 + 8, 2 * LANES : 2 * LANES + 128]
            bias = bias.reshape(chips, 1, units // 2)
            bias = jnp.pad(
                bias, ((0, 0), (8, LINES - 9), (0, side - 2 * LANES - units // 2))
            )
            lines = jnp.concatenate([slim.reshape(chips, LINES, 2 * LANES), bias], axis=2)
            whole = jnp.concatenate([square, lines], axis=1)
            share_one = lax.psum_scatter(whole, "dp", axis_index_groups=same_core).astype(WIDE)

        split = share_two[: 2 * depth].reshape(2, depth, width).astype(SHORT)
        own, other = pick(split, core, 0), swap_core(pick(split, 1 - core, 0))
        own_down = share_three.astype(SHORT)
        moved_down = swap_seq(own_down)
        moved = swap_seq(jnp.concatenate([own, other], axis=0))
        pair_two = own, other, moved
        split = share_one[: 2 * depth].reshape(2, depth, side).astype(SHORT)
        lines = share_one[2 * depth :, : 2 * LANES].reshape(LINES, 2, LANES)
        packet = jnp.pad(pick(lines, 1 - core, 1).astype(SHORT), ((0, 0), (0, side - LANES)))
        other = swap_core(jnp.concatenate([pick(split, 1 - core, 0), packet], axis=0))
        own = pick(split, core, 0)
        line = pick(lines, core, 1) + other[depth:, :LANES].astype(WIDE)
        bias = share_one[2 * depth + 8, 2 * LANES : 2 * LANES + units // 2]
        packet = jnp.concatenate(
            [line.astype(SHORT), share_one[2 * depth :, 2 * LANES :].astype(SHORT)], axis=1
        )
        packet = jnp.pad(packet, ((0, 0), (0, LANES)))
        packet = jnp.concatenate([own, other[:depth], packet], axis=0)
        own_two, other_two, moved_two = after(packet, *pair_two)
        moved = swap_seq(packet)
        by_chip = (depth, chips, units // 2)
        near = in_order(core, own_two.reshape(by_chip), other_two.reshape(by_chip), 2)
        away = in_order(
            core, moved_two[:depth].reshape(by_chip), moved_two[depth : 2 * depth].reshape(by_chip), 2
        )
        final_up = in_order(half, near, away, 3).reshape(depth, tall).astype(WIDE)
        final_down = in_order(half, own_down, moved_down, 0)
        final_down = final_down.reshape(units, width).astype(WIDE)

        by_third = (depth, 3, quarter)
        near = in_order(
            core,
            own[:, : 3 * quarter].reshape(by_third),
            other[:depth, : 3 * quarter].reshape(by_third),
            2,
        )
        away = in_order(
            core,
            moved[:depth, : 3 * quarter].reshape(by_third),
            moved[depth : 2 * depth, : 3 * quarter].reshape(by_third),
            2,
        )
        final_qkv = in_order(half, near, away, 2).reshape(depth, 3 * width).astype(WIDE)
        near = own[:, 3 * quarter :].astype(WIDE) + moved[:depth, 3 * quarter :].astype(WIDE)
        away = other[:depth, 3 * quarter :].astype(WIDE) + moved[
            depth : 2 * depth, 3 * quarter :
        ].astype(WIDE)
        final_out = in_order(core, near, away, 1).reshape(depth, width)
        line = line + moved[2 * depth :, :LANES].astype(WIDE)
        finals = [line[i, :depth] for i in range(8)]
        from_seq = moved[2 * depth + 8, LANES : LANES + units // 2].astype(WIDE)
        final_bias = in_order(half, bias, from_seq, 0).reshape(-1)

        return (
            layer_out.reshape(inputs.shape),
            input_grad.reshape(inputs.shape),
            final_qkv,
            final_out,
            final_up,
            final_down,
            finals[0],
            finals[1],
            finals[2],
            finals[3],
            finals[4],
            final_bias,
            finals[5],
            finals[6],
            finals[7],
        )

    return per_device


def solution(mesh):
    token = P(None, ("dp", "seq"), None)
    matrix = P("dp", None)
    vector = P("dp")
    placed = (token, token) + (matrix,) * 4 + (vector,) * 9
    return jax.shard_map(
        build(mesh), mesh=mesh, in_specs=placed, out_specs=placed, check_vma=False
    )
```

```python
import functools
import math

import jax
import jax.numpy as jnp
from jax import lax
from jax.experimental import pallas as pl
from jax.experimental.pallas import tpu as pltpu
from jax.sharding import PartitionSpec as P

HEAD = 64
CORES = 2
PARTS = 8
SHORT = jnp.bfloat16
WIDE = jnp.float32
LIMIT = 12 * 1024 * 1024
WHOLE = 56 * 1024 * 1024
LINES = 16
LANES = 256


def gelu_exact(values):
    return 0.5 * values * (1.0 + lax.erf(values * (1.0 / math.sqrt(2.0))))


def gelu_slope(values):
    bell = jnp.exp(values * values * -0.5) * (1.0 / math.sqrt(2.0 * math.pi))
    return 0.5 * (1.0 + lax.erf(values * (1.0 / math.sqrt(2.0)))) + values * bell


def times(left, right):
    return jnp.dot(left, right, preferred_element_type=WIDE)


def times_back(left, right):
    return lax.dot_general(left, right, (((1,), (1,)), ((), ())), preferred_element_type=WIDE)


def inner_rows(left, right):
    return lax.dot_general(left, right, (((0,), (0,)), ((), ())), preferred_element_type=WIDE)


def column_sum(part):
    return jnp.sum(part, axis=0, keepdims=True)


def standard(features):
    centre = jnp.mean(features, axis=-1, keepdims=True)
    centred = features - centre
    spread = jnp.mean(centred * centred, axis=-1, keepdims=True)
    slope = lax.rsqrt(spread + 1e-12)
    return centred * slope, slope


def standard_back(normal, slope, grad):
    even = jnp.mean(grad, axis=-1, keepdims=True)
    along = jnp.mean(normal * grad, axis=-1, keepdims=True)
    return slope * (grad - even - normal * along)


def pick(array, index, axis):
    return lax.dynamic_index_in_dim(array, index, axis, keepdims=False)


def in_order(place, own, other, axis):
    first = place == 0
    return jnp.stack([jnp.where(first, own, other), jnp.where(first, other, own)], axis=axis)


def block(index, size):
    return pl.ds(pl.multiple_of(index * size, size), size)


def here():
    index = lax.axis_index("dp")
    return lax.div(index, CORES), lax.rem(index, CORES), lax.axis_index("seq")


def part_index(step, flip, ringed, chip, chips):
    if not ringed:
        return step
    half = chips // 2
    upper = lax.rem(chip, 2)
    level = lax.div(chip, 2)
    spot = jnp.where(upper == 0, level, chips - 1 - level)
    away = (step + 1) // 2
    sign = -1 if (step % 2 == 1) != flip else 1
    spot = lax.rem(spot + sign * away + chips, chips)
    return jnp.where(spot < half, 2 * spot, 2 * (chips - 1 - spot) + 1)


def call(body, outs, scratch=(), flops=0, moved=0, limit=LIMIT):
    return pl.pallas_call(
        body,
        out_shape=[jax.ShapeDtypeStruct(shape, kind) for shape, kind in outs],
        scratch_shapes=[pltpu.VMEM(shape, kind) for shape, kind in scratch],
        compiler_params=pltpu.CompilerParams(vmem_limit_bytes=limit),
        cost_estimate=pl.CostEstimate(flops=flops, bytes_accessed=moved, transcendentals=0),
    )


def pack_kernel(*refs):
    vectors, up_bias, w_qkv, w_out, mine, theirs = refs[:8], *refs[8:]
    _, core, half = here()
    depth = w_qkv.shape[0]
    width = w_out.shape[1]
    quarter = width // 4
    for out, which in ((mine, core), (theirs, 1 - core)):
        for third in range(3):
            start = third * width + (2 * half + which) * quarter
            out[:depth, third * quarter : (third + 1) * quarter] = w_qkv[
                :, pl.ds(pl.multiple_of(start, quarter), quarter)
            ]
        out[:depth, 3 * quarter :] = w_out[:, block(which, width // 2)]
        lines = [
            jnp.pad(vector[...], ((0, 0), (0, LANES - depth))).astype(WIDE) for vector in vectors
        ]
        lines.append(jnp.pad(up_bias[...].astype(WIDE), ((0, 0), (0, LANES - up_bias.shape[1]))))
        lines.append(jnp.zeros((LINES - 9, LANES), WIDE))
        out[depth:, :LANES] = jnp.concatenate(lines, axis=0).astype(SHORT)
        out[depth:, LANES:] = jnp.zeros((LINES, out.shape[1] - LANES), SHORT)


def heads_of(qkv, rows, head, quarter):
    return [
        qkv[rows, third * quarter + head * HEAD : third * quarter + (head + 1) * HEAD]
        for third in range(3)
    ]


def softmax(queries, keys, scale):
    scores = times_back(queries, keys) * scale
    expo = jnp.exp(scores - jnp.max(scores, axis=-1, keepdims=True))
    return expo / jnp.sum(expo, axis=-1, keepdims=True)


def fill_group(group, pieces, micro):
    rows = pieces[0].shape[0] // micro
    for place in range(4 * micro):
        far, item, side = place // (2 * micro), place // 2 % micro, place % 2
        group[place * rows : (place + 1) * rows, :] = pieces[2 * far + side][
            item * rows : (item + 1) * rows, :
        ]


def attention_kernel(micro, where, *refs):
    pieces, chunks, rest = refs[:4], refs[4:13], refs[13:]
    tokens, full, qkv, keep, send, kept, vectors, up_bias, out_half, wide = rest
    chip, core, half = here()
    quarter = keep.shape[1]
    scale = 1.0 / math.sqrt(HEAD)
    fill_group(tokens, pieces, micro)
    for step in range(PARTS):
        spot = block(where(step, chip), 128)
        chunk, start = chunks[step], 128
        if step < PARTS - 1:
            full[spot, :] = chunk[:128, : 3 * quarter]
            out_half[spot, :] = chunk[:128, 3 * quarter :]
        else:
            for side in range(2):
                piece = chunks[step + side]
                inner = block(2 * where(step, chip) + side, 64)
                full[inner, :] = piece[:64, : 3 * quarter]
                out_half[inner, :] = piece[:64, 3 * quarter :]
            chunk, start = piece, 64
        lines = jnp.concatenate([chunk[start:, :64], chunk[start:, LANES : LANES + 64]], axis=1)
        vectors[:, spot] = lines.astype(WIDE)
        lines = chunk[start:, block(core * (LANES // 128) + half, 128)]
        up_bias[:, spot] = lines.astype(WIDE)[8:9, :]
    wide[...] = times(tokens[...], full[...])
    spot = block(2 * half + core, quarter)
    qkv[:, :quarter] = (wide[:, :quarter] + vectors[0:1, spot]).astype(SHORT)
    qkv[:, quarter : 2 * quarter] = wide[:, quarter : 2 * quarter].astype(SHORT)
    qkv[:, 2 * quarter :] = (wide[:, 2 * quarter :] + vectors[1:2, spot]).astype(SHORT)
    length = tokens.shape[0] // (2 * micro)
    rows = length // 2
    for item in range(2 * micro):
        for pair in range(quarter // 128):
            both = []
            for head in (2 * pair, 2 * pair + 1):
                queries, keys, values = heads_of(
                    qkv, slice(item * length, (item + 1) * length), head, quarter
                )
                probs = softmax(queries, keys, scale)
                kept[item * (quarter // HEAD) + head] = probs
                both.append(times(probs.astype(SHORT), values))
            both = jnp.concatenate(both, axis=1).astype(SHORT)
            spot = slice(pair * 128, (pair + 1) * 128)
            keep[item * rows : (item + 1) * rows, spot] = both[:rows]
            send[item * rows : (item + 1) * rows, spot] = both[rows:]


def first_kernel(
    inputs, keep, from_seq, from_core, mine, other, vectors, resid, first, low, context
):
    _, core, half = here()
    rows, width = inputs.shape
    quarter = width // 4
    flip_core, flip_half = 1 - core, 1 - half
    context[:, block(2 * half + core, quarter)] = keep[:rows, :]
    context[:, block(2 * flip_half + core, quarter)] = from_seq[:rows, :]
    context[:, block(2 * half + flip_core, quarter)] = from_core[:, :quarter]
    context[:, block(2 * flip_half + flip_core, quarter)] = from_core[:, quarter:]
    whole = context[...]
    resid[:, block(core, width // 2)] = times(whole, mine[...])
    resid[:, block(flip_core, width // 2)] = times(whole, other[...])
    features = inputs[...].astype(WIDE) + (resid[...] + vectors[2:3, :])
    resid[...] = features
    normal, _ = standard(features)
    features = normal * vectors[3:4, :] + vectors[4:5, :]
    first[...] = features
    low[...] = features.astype(SHORT)


def split_rows(value, start, micro, rows, keep, send):
    for place in range(value.shape[0] // rows):
        far, item, side = (
            (start + place * rows) // rows // (2 * micro),
            (start + place * rows) // rows // 2 % micro,
            (start + place * rows) // rows % 2,
        )
        part = value[place * rows : (place + 1) * rows, :]
        if far:
            send[side, item * rows : (item + 1) * rows, :] = part.astype(SHORT)
        else:
            keep[side, item * rows : (item + 1) * rows, :] = part


def forward_kernel(micro, where, *refs):
    pieces, chunks, up_bias, rest = refs[:4], refs[4:22], refs[22], refs[23:]
    group, full_up, full_down, pre_act, act, keep, send = rest
    chip, _, _ = here()
    fill_group(group, pieces, micro)
    for full, parts in ((full_up, chunks[:9]), (full_down, chunks[9:])):
        for step in range(PARTS - 1):
            full[block(where(step, chip), 128), :] = parts[step][...]
        for side in range(2):
            full[block(2 * where(PARTS - 1, chip) + side, 64), :] = parts[PARTS - 1 + side][...]
    rows = pieces[0].shape[0] // micro
    tall = group.shape[0] // 2
    for side in range(2):
        spot = slice(side * tall, (side + 1) * tall)
        pre = times(group[spot, :], full_up[...]) + up_bias[...]
        pre_act[spot, :] = pre
        act[spot, :] = gelu_exact(pre).astype(SHORT)
        out = times(act[spot, :], full_down[...])
        split_rows(out, side * tall, micro, rows, keep, send)


def slope_kernel(pre_act, slope):
    for start in range(0, pre_act.shape[0], 64):
        slope[start : start + 64, :] = gelu_slope(pre_act[start : start + 64, :])


def second_kernel(
    first, keep, from_core, from_seq, vectors, cotangent, out, grad, low, sums
):
    mlp = keep[0] + from_core[0].astype(WIDE) + from_seq[...].astype(WIDE)
    normal, slope = standard(first[...] + (mlp + vectors[5:6, :]))
    out[...] = (normal * vectors[6:7, :] + vectors[7:8, :]).astype(SHORT)
    incoming = cotangent[...].astype(WIDE)
    resid = standard_back(normal, slope, incoming * vectors[6:7, :])
    grad[...] = resid
    short = resid.astype(SHORT)
    low[...] = short
    sums[...] = jnp.zeros_like(sums)
    sums[0:1, :] = column_sum(short.astype(WIDE))
    sums[1:2, :] = column_sum(incoming * normal)
    sums[2:3, :] = column_sum(incoming)


def backward_kernel(micro, where, *refs):
    pieces, rest = refs[:4], refs[4:]
    group, full_up, full_down, slopes, act, chunks_up, chunks_down, keep, send, sums, grad, pre = rest
    chip, _, _ = here()
    fill_group(grad, pieces, micro)
    rows = pieces[0].shape[0] // micro
    tall = grad.shape[0] // 2
    total = None
    for side in range(2):
        spot = slice(side * tall, (side + 1) * tall)
        part = (times_back(grad[spot, :], full_down[...]) * slopes[spot, :]).astype(SHORT)
        pre[spot, :] = part
        part = column_sum(part.astype(WIDE))
        total = part if total is None else total + part
    sums[...] = total
    for step in range(PARTS):
        spot = block(where(step, chip), 128)
        chunks_down[step] = inner_rows(act[:, spot], grad[...]).astype(SHORT)
        chunks_up[step] = inner_rows(group[:, spot], pre[...]).astype(SHORT)
    for side in range(2):
        spot = slice(side * tall, (side + 1) * tall)
        out = times_back(pre[spot, :], full_up[...])
        split_rows(out, side * tall, micro, rows, keep, send)


def first_back_kernel(
    resid,
    grad_two,
    keep,
    from_core,
    from_seq,
    vectors,
    context,
    mine,
    other,
    grad,
    out_keep,
    out_send,
    ctx_keep,
    ctx_send,
    sums,
):
    _, core, half = here()
    width = resid.shape[1]
    quarter = width // 4
    incoming = grad_two[...] + (keep[0] + from_core[0].astype(WIDE) + from_seq[...].astype(WIDE))
    normal, slope = standard(resid[...])
    value = standard_back(normal, slope, incoming * vectors[3:4, :])
    grad[...] = value
    short = value.astype(SHORT)
    sums[...] = jnp.zeros_like(sums)
    sums[0:1, :] = column_sum(short.astype(WIDE))
    sums[1:2, :] = column_sum(incoming * normal)
    sums[2:3, :] = column_sum(incoming)
    left, right = short[:, : width // 2], short[:, width // 2 :]
    own = jnp.where(core == 0, left, right)
    away = jnp.where(core == 0, right, left)
    out_keep[...] = inner_rows(context[...], own).astype(SHORT)
    out_send[...] = inner_rows(context[...], away).astype(SHORT)
    for target, which in ((ctx_keep, core), (ctx_send, 1 - core)):
        for side, which_half in enumerate((half, 1 - half)):
            spot = block(2 * which_half + which, quarter)
            value = times_back(own, mine[spot, :]) + times_back(away, other[spot, :])
            target[:, side * quarter : (side + 1) * quarter] = value.astype(SHORT)


def attention_back_kernel(micro, where, *refs):
    qkv, kept, ctx_keep, ctx_core, ctx_seq, tokens, out_keep, out_core = refs[:8]
    sums_two, sums_one, up_sums, chunks, grad, flag, vectors = refs[8:]
    chip, core, half = here()
    quarter = qkv.shape[1] // 3
    length = qkv.shape[0] // (2 * micro)
    rows = length // 2
    scale = 1.0 / math.sqrt(HEAD)
    for item in range(2 * micro):
        spot = slice(item * length, (item + 1) * length)
        near = ctx_keep if item < micro else ctx_core
        inner = slice(item % micro * rows, (item % micro + 1) * rows)
        outer = slice(item * rows, (item + 1) * rows)
        for pair in range(quarter // 128):
            lanes = slice(pair * 128, (pair + 1) * 128)
            incoming = jnp.concatenate([near[inner, lanes], ctx_seq[outer, lanes]], axis=0)
            results = [[], [], []]
            for side in range(2):
                queries, keys, values = heads_of(qkv, spot, 2 * pair + side, quarter)
                probs = kept[item * (quarter // HEAD) + 2 * pair + side]
                own = incoming[:, side * HEAD : (side + 1) * HEAD]
                grad_probs = times_back(own, values)
                along = jnp.sum(probs * grad_probs, axis=-1, keepdims=True)
                grad_scores = (probs * (grad_probs - along)).astype(SHORT)
                results[0].append(times(grad_scores, keys) * scale)
                results[1].append(inner_rows(grad_scores, queries) * scale)
                results[2].append(inner_rows(probs.astype(SHORT), own))
            for third in range(3):
                start = third * quarter + pair * 128
                grad[spot, start : start + 128] = jnp.concatenate(results[third], axis=1).astype(
                    SHORT
                )
    line = column_sum(grad[...].astype(WIDE))
    vectors[...] = jnp.zeros_like(vectors)
    vectors[0:1, block(2 * half + core, quarter)] = line[:, :quarter]
    vectors[1:2, block(2 * half + core, quarter)] = line[:, 2 * quarter :]
    vectors[2:5, :] = sums_one[0:3, :]
    vectors[5:8, :] = sums_two[0:3, :]
    vectors[8:9, :] = up_sums[...]
    flag[...] = vectors[0:8, 0:128]
    for step in range(PARTS):
        spot = block(where(step, chip), 128)
        chunks[step, :128, : 3 * quarter] = inner_rows(tokens[:, spot], grad[...]).astype(SHORT)
        chunks[step, :128, 3 * quarter :] = (
            out_keep[spot, :].astype(WIDE) + out_core[spot, :].astype(WIDE)
        ).astype(SHORT)
        lines = vectors[:, spot].astype(SHORT)
        chunks[step, 128:, :] = jnp.zeros((LINES, chunks.shape[2]), SHORT)
        chunks[step, 128:, :64] = lines[:, :64]
        chunks[step, 128:, LANES : LANES + 64] = lines[:, 64:]
        chunks[step, 128:, 2 * LANES : 2 * LANES + 128] = lines


def input_back_kernel(micro, rows, grad, full, keep, send):
    tall = grad.shape[0] // 2
    for side in range(2):
        out = times_back(grad[side * tall : (side + 1) * tall, :], full[...])
        split_rows(out, side * tall, micro, rows, keep, send)


def final_kernel(own, other, moved, line, grad_qkv, grad_out, total):
    _, core, half = here()
    depth, width = grad_out.shape
    quarter = width // 4
    flip_core, flip_half = 1 - core, 1 - half
    sources = (
        (own[...], half, core),
        (other[:depth, :], half, flip_core),
        (moved[:depth, :], flip_half, core),
        (moved[depth : 2 * depth, :], flip_half, flip_core),
    )
    for value, side, which in sources:
        for third in range(3):
            spot = block(4 * third + 2 * side + which, quarter)
            grad_qkv[:, spot] = value[:, third * quarter : (third + 1) * quarter].astype(WIDE)
    parts = [value[:, 3 * quarter :].astype(WIDE) for value, _, _ in sources]
    grad_out[:, block(core, width // 2)] = parts[0] + parts[2]
    grad_out[:, block(flip_core, width // 2)] = parts[1] + parts[3]
    total[...] = line[...] + moved[2 * depth :, :LANES].astype(WIDE)


def after(gate, *values):
    if gate is None:
        return values
    return lax.optimization_barrier((*values, gate))[:-1]


def build(mesh):
    devices = mesh.shape["dp"]
    chips = devices // CORES
    ringed = chips == PARTS
    half_ring = chips // 2
    ring = [2 * i for i in range(half_ring)] + [2 * i + 1 for i in reversed(range(half_ring))]
    same_core = [list(range(core, devices, CORES)) for core in range(CORES)]
    core_pairs = [(i, i ^ 1) for i in range(devices)]

    def hop(step):
        return [
            (ring[i] * CORES + core, ring[(i + step) % chips] * CORES + core)
            for i in range(chips)
            for core in range(CORES)
        ]

    onward, backward = hop(1), hop(-1)

    def swap_core(array):
        return lax.ppermute(array, "dp", core_pairs)

    def swap_seq(array):
        return lax.ppermute(array, "seq", [(0, 1), (1, 0)])

    def gather_ring(chunk, cut, flip, gates=(None, None, None)):
        far, near = (backward, onward) if flip else (onward, backward)
        got = [chunk]
        one = two = chunk
        for step in range(chips // 2 - 1):
            if step:
                one, two = after(gates[step - 1], one, two)
            one = lax.ppermute(one, "dp", far)
            two = lax.ppermute(two, "dp", near)
            got += [one, two]
        one, two = after(gates[-1], one, two)
        return got + [lax.ppermute(one[:cut], "dp", far), lax.ppermute(two[cut:], "dp", near)]

    def sum_ring(parts, cut, flip, gates=(None, None, None)):
        far, near = (onward, backward) if flip else (backward, onward)
        last = parts[chips - 1]
        one, two = last[:cut], last[cut:]
        for step in range(chips // 2 - 1):
            one = lax.ppermute(one, "dp", far)
            two = lax.ppermute(two, "dp", near)
            one, two = after(gates[step], one, two)
            one, two = one.astype(WIDE), two.astype(WIDE)
            place = chips - 3 - 2 * step
            here, there = parts[place].astype(WIDE), parts[place + 1].astype(WIDE)
            if step:
                one, two = one + here, two + there
            else:
                one = jnp.concatenate([one + here[:cut], here[cut:]], axis=0)
                two = jnp.concatenate([there[:cut], two + there[cut:]], axis=0)
            one, two = one.astype(SHORT), two.astype(SHORT)
        one = lax.ppermute(one, "dp", far)
        two = lax.ppermute(two, "dp", near)
        return one.astype(WIDE) + two.astype(WIDE) + parts[0].astype(WIDE)

    def where(flip, step, chip):
        return part_index(step, flip, ringed, chip, chips)

    where_one = functools.partial(where, False)
    where_two = functools.partial(where, True)

    def per_device(
        inputs,
        cotangent,
        w_qkv,
        w_out,
        w_up,
        w_down,
        bias_q,
        bias_v,
        bias_out,
        gain_one,
        shift_one,
        bias_up,
        bias_down,
        gain_two,
        shift_two,
    ):
        index = lax.axis_index("dp")
        core = index % CORES
        half = lax.axis_index("seq")
        micro, rows, width = inputs.shape
        own_rows = micro * rows
        group = 4 * own_rows
        depth = w_qkv.shape[0]
        units = w_down.shape[0]
        tall = w_up.shape[1]
        quarter = width // 4
        side = 3 * quarter + width // 2
        several = chips // PARTS

        def share(own):
            from_seq = swap_seq(own)
            return own, from_seq, swap_core(own), swap_core(from_seq)

        def finish_sum(keep, from_core):
            moving = (keep[1] + from_core[1].astype(WIDE)).astype(SHORT)
            return swap_seq(moving)

        vectors = (
            bias_q,
            bias_v,
            bias_out,
            gain_one,
            shift_one,
            bias_down,
            gain_two,
            shift_two,
            bias_up,
        )
        mine, theirs = call(pack_kernel, [((depth + LINES, side), SHORT)] * 2, moved=10**6, limit=WHOLE)(
            *[vector.reshape(1, -1) for vector in vectors], w_qkv, w_out
        )
        theirs = swap_core(theirs)
        square = in_order(core, mine[:depth], theirs[:depth], 0).reshape(2 * depth, side)
        lines = in_order(core, mine[depth:, :LANES], theirs[depth:, :LANES], 1)
        lines = jnp.pad(lines.reshape(LINES, 2 * LANES), ((0, 0), (0, side - 2 * LANES)))
        chunk_one = jnp.concatenate([square, lines], axis=0)

        by_unit = w_up.reshape(depth, chips, 2, 2, units // 2)
        by_unit = pick(by_unit, half, 3)
        mine = pick(by_unit, core, 2).reshape(depth, tall // 4)
        theirs = pick(by_unit, 1 - core, 2).reshape(depth, tall // 4)
        both = in_order(core, mine, swap_core(theirs), 0).reshape(2 * depth, tall // 4)
        own_down = pick(w_down.reshape(2, units // 2, width), half, 0)
        chunk_two, chunk_three = both, own_down

        flat = inputs.reshape(own_rows, width)
        shared = share(flat)
        if ringed:
            chunks_one = gather_ring(chunk_one, 64, False, (chunk_two, shared[1], None))
            chunk_two, chunk_three = after(chunks_one[5], chunk_two, chunk_three)
        else:
            whole = lax.all_gather(chunk_one, "dp", axis_index_groups=same_core)
            square = whole[:, : 2 * depth].reshape(PARTS, 128, side)
            lines = whole[:, 2 * depth :, : 2 * LANES].reshape(chips, LINES, 2, LANES)
            slim = lines[:, :8, :, :depth].reshape(PARTS, several, 8, 2 * depth)
            slim = slim.transpose(0, 2, 1, 3).reshape(PARTS, 8, 2, 64)
            slim = jnp.pad(slim, ((0, 0), (0, 0), (0, 0), (0, LANES - 64)))
            slim = slim.reshape(PARTS, 8, 2 * LANES)
            bias = pick(lines[:, 8, :, :units], core, 1).reshape(chips, 2, units // 2)
            bias = pick(bias, half, 1).reshape(PARTS, 1, 128)
            lines = jnp.concatenate([slim, jnp.tile(bias, (1, 1, 2 * LANES // 128))], axis=1)
            lines = jnp.pad(lines, ((0, 0), (0, LINES - 9), (0, side - 2 * LANES)))
            whole = jnp.concatenate([square, lines], axis=1)
            chunks_one = [whole[step] for step in range(PARTS - 1)]
            chunks_one += [whole[-1, :64], whole[-1, 64:]]
            chunks_two = []
            for chunk in (chunk_two, chunk_three):
                whole = lax.all_gather(chunk, "dp", axis_index_groups=same_core)
                whole = whole.reshape(PARTS, 128, width)
                chunks_two += [whole[step] for step in range(PARTS - 1)]
                chunks_two += [whole[-1, :64], whole[-1, 64:]]

        tokens, full_qkv, qkv, ctx_keep, ctx_send, probs, table, up_bias, out_mine = call(
            functools.partial(attention_kernel, micro, where_one),
            [
                ((group, width), SHORT),
                ((width, 3 * quarter), SHORT),
                ((group, 3 * quarter), SHORT),
                ((group // 2, quarter), SHORT),
                ((group // 2, quarter), SHORT),
                ((2 * micro * quarter // HEAD, 2 * rows, 2 * rows), WIDE),
                ((LINES, width), WIDE),
                ((1, tall // 4), WIDE),
                ((width, width // 2), SHORT),
            ],
            [((group, 3 * quarter), WIDE)],
            flops=2 * group * width * width,
            moved=8 * 10**6,
        )(*shared, *chunks_one)
        out_other = swap_core(out_mine)
        ctx_seq = swap_seq(ctx_send)
        ctx_core = swap_core(
            jnp.concatenate([ctx_keep[own_rows:], ctx_seq[own_rows:]], axis=1)
        )
        resid, first, first_low, context = call(
            first_kernel,
            [
                ((own_rows, width), WIDE),
                ((own_rows, width), WIDE),
                ((own_rows, width), SHORT),
                ((own_rows, width), SHORT),
            ],
            flops=2 * own_rows * width * width,
            moved=4 * 10**6,
        )(flat, ctx_keep, ctx_seq, ctx_core, out_mine, out_other, table)

        pieces = share(first_low)
        if ringed:
            gates = (ctx_seq, pieces[1], None)
            chunks_two = gather_ring(chunk_two, 64, True, gates)
            chunks_two += gather_ring(chunk_three, 64, True, gates)
        split_out = [((2, own_rows, width), WIDE), ((2, own_rows, width), SHORT)]
        first_group, full_up, full_down, pre_act, act, keep, send = call(
            functools.partial(forward_kernel, micro, where_two),
            [
                ((group, width), SHORT),
                ((width, tall // 4), SHORT),
                ((tall // 4, width), SHORT),
                ((group, tall // 4), WIDE),
                ((group, tall // 4), SHORT),
            ]
            + split_out,
            flops=group * width * tall,
            moved=16 * 10**6,
        )(*pieces, *chunks_two, up_bias)
        from_core = swap_core(send)
        moving = (keep[1] + from_core[1].astype(WIDE)).astype(SHORT)
        (pre_act,) = after(moving, pre_act)
        (slopes,) = call(slope_kernel, [((group, tall // 4), WIDE)], moved=5 * 10**6)(pre_act)
        from_seq = swap_seq(moving)
        layer_out, grad_two, mlp_low, sums_two = call(
            second_kernel,
            [
                ((own_rows, width), SHORT),
                ((own_rows, width), WIDE),
                ((own_rows, width), SHORT),
                ((8, width), WIDE),
            ],
            moved=3 * 10**6,
        )(first, keep, from_core, from_seq, table, cotangent.reshape(own_rows, width))

        grads_two, grads_three, keep, send, up_sums = call(
            functools.partial(backward_kernel, micro, where_two),
            [((PARTS, 128, width), SHORT)] * 2 + split_out + [((1, tall // 4), WIDE)],
            [((group, width), SHORT), ((group, tall // 4), SHORT)],
            flops=2 * group * width * tall,
            moved=16 * 10**6,
        )(*share(mlp_low), first_group, full_up, full_down, slopes, act)
        from_core = swap_core(send)
        from_seq = finish_sum(keep, from_core)
        gate_one = from_seq
        grad_one, out_keep, out_send, grad_keep, grad_send, sums_one = call(
            first_back_kernel,
            [
                ((own_rows, width), WIDE),
                ((width, width // 2), SHORT),
                ((width, width // 2), SHORT),
                ((own_rows, width // 2), SHORT),
                ((own_rows, width // 2), SHORT),
                ((8, width), WIDE),
            ],
            flops=4 * own_rows * width * width,
            moved=8 * 10**6,
        )(resid, grad_two, keep, from_core, from_seq, table, context, out_mine, out_other)
        grad_core = swap_core(grad_send)
        grad_seq = swap_seq(jnp.concatenate([grad_keep[:, quarter:], grad_core[:, quarter:]]))
        out_core = swap_core(out_send)
        grads_one, grad_tokens, flag = call(
            functools.partial(attention_back_kernel, micro, where_one),
            [
                ((PARTS, 128 + LINES, side), SHORT),
                ((group, 3 * quarter), SHORT),
                ((8, 128), WIDE),
            ],
            [((LINES, width), WIDE)],
            flops=3 * group * width * width,
            moved=12 * 10**6,
        )(
            qkv,
            probs,
            grad_keep,
            grad_core,
            grad_seq,
            tokens,
            out_keep,
            out_core,
            sums_two,
            sums_one,
            up_sums,
        )
        keep, send = call(
            functools.partial(input_back_kernel, micro, rows),
            split_out,
            flops=group * width * width,
            moved=5 * 10**6,
        )(grad_tokens, full_qkv)
        from_core = swap_core(send)
        moving = (keep[1] + from_core[1].astype(WIDE)).astype(SHORT)
        from_seq = swap_seq(moving)
        gates_one = (moving, from_seq, None)
        input_grad = grad_one + (keep[0] + from_core[0].astype(WIDE) + from_seq.astype(WIDE))

        if ringed:
            share_three = sum_ring(grads_three, 64, True, (gate_one, flag, None))
            share_two = sum_ring(grads_two, 64, True, (gate_one, grad_seq, flag))
            share_one = sum_ring(grads_one, 64, False, gates_one)
        else:
            whole = grads_three.reshape(chips, units // 2, width)
            share_three = lax.psum_scatter(whole, "dp", axis_index_groups=same_core).astype(WIDE)
            whole = grads_two.reshape(chips, 2 * depth, width)
            share_two = lax.psum_scatter(whole, "dp", axis_index_groups=same_core).astype(WIDE)
            square = grads_one[:, :128].reshape(chips, 2 * depth, side)
            slim = grads_one[:, 128 : 128 + 8, : 2 * LANES].reshape(PARTS, 8, 2, LANES)[..., :64]
            slim = slim.reshape(PARTS, 8, several, 2 * depth).transpose(0, 2, 1, 3)
            slim = slim.reshape(chips, 8, 2, depth)
            slim = jnp.pad(slim, ((0, 0), (0, LINES - 8), (0, 0), (0, LANES - depth)))
            bias = grads_one[:, 128 + 8, 2 * LANES : 2 * LANES + 128]
            bias = bias.reshape(chips, 1, units // 2)
            bias = jnp.pad(
                bias, ((0, 0), (8, LINES - 9), (0, side - 2 * LANES - units // 2))
            )
            lines = jnp.concatenate([slim.reshape(chips, LINES, 2 * LANES), bias], axis=2)
            whole = jnp.concatenate([square, lines], axis=1)
            share_one = lax.psum_scatter(whole, "dp", axis_index_groups=same_core).astype(WIDE)

        split = share_two[: 2 * depth].reshape(2, depth, width).astype(SHORT)
        own, other = pick(split, core, 0), swap_core(pick(split, 1 - core, 0))
        own_down = share_three.astype(SHORT)
        moved_down = swap_seq(own_down)
        moved = swap_seq(jnp.concatenate([own, other], axis=0))
        pair_two = own, other, moved
        split = share_one[: 2 * depth].reshape(2, depth, side).astype(SHORT)
        lines = share_one[2 * depth :, : 2 * LANES].reshape(LINES, 2, LANES)
        packet = jnp.pad(pick(lines, 1 - core, 1).astype(SHORT), ((0, 0), (0, side - LANES)))
        other = swap_core(jnp.concatenate([pick(split, 1 - core, 0), packet], axis=0))
        own = pick(split, core, 0)
        line = pick(lines, core, 1) + other[depth:, :LANES].astype(WIDE)
        bias = share_one[2 * depth + 8, 2 * LANES : 2 * LANES + units // 2]
        packet = jnp.concatenate(
            [line.astype(SHORT), share_one[2 * depth :, 2 * LANES :].astype(SHORT)], axis=1
        )
        packet = jnp.pad(packet, ((0, 0), (0, LANES)))
        packet = jnp.concatenate([own, other[:depth], packet], axis=0)
        own_two, other_two, moved_two = after(packet, *pair_two)
        moved = swap_seq(packet)
        by_chip = (depth, chips, units // 2)
        near = in_order(core, own_two.reshape(by_chip), other_two.reshape(by_chip), 2)
        away = in_order(
            core, moved_two[:depth].reshape(by_chip), moved_two[depth : 2 * depth].reshape(by_chip), 2
        )
        final_up = in_order(half, near, away, 3).reshape(depth, tall).astype(WIDE)
        final_down = in_order(half, own_down, moved_down, 0)
        final_down = final_down.reshape(units, width).astype(WIDE)

        final_qkv, final_out, line = call(
            final_kernel,
            [((depth, 3 * width), WIDE), ((depth, width), WIDE), ((LINES, LANES), WIDE)],
            moved=2 * 10**6,
        )(own, other, moved, line)
        finals = [line[i, :depth] for i in range(8)]
        from_seq = moved[2 * depth + 8, LANES : LANES + units // 2].astype(WIDE)
        final_bias = in_order(half, bias, from_seq, 0).reshape(-1)

        return (
            layer_out.reshape(inputs.shape),
            input_grad.reshape(inputs.shape),
            final_qkv,
            final_out,
            final_up,
            final_down,
            finals[0],
            finals[1],
            finals[2],
            finals[3],
            finals[4],
            final_bias,
            finals[5],
            finals[6],
            finals[7],
        )

    return per_device


def solution(mesh):
    token = P(None, ("dp", "seq"), None)
    matrix = P("dp", None)
    vector = P("dp")
    placed = (token, token) + (matrix,) * 4 + (vector,) * 9
    return jax.shard_map(
        build(mesh), mesh=mesh, in_specs=placed, out_specs=placed, check_vma=False
    )
```
